256 devices in a mesh: context: 32 (over z, x), ulysses: 4 (over y), dp: 2 (over core).
Axes of the slice: x: 4, y: 4, z: 8, core: 2. Of those that a mesh axis runs over, the one named last changes fastest.
Arguments:
- queries: bfloat16 [32768, 4096], P(('dp', 'context', 'ulysses')), parts along dimension 0, may hold values from -5 to 5
- keys: bfloat16 [32768, 512], P(('dp', 'context', 'ulysses')), parts along dimension 0, may hold values from -5 to 5
- values: bfloat16 [32768, 512], P(('dp', 'context', 'ulysses')), parts along dimension 0, may hold values from -6 to 6
- segments: int32 [32768], P(('dp', 'context')), parts along dimension 0, may hold values from 0 to 63, never falling along the last dimension, each value on 1 to 4096 neighbouring positions
- feat_q: bfloat16 [32, 128, 128], P('ulysses'), may hold values from -2 to 2
- feat_k: bfloat16 [4, 128, 128], P('ulysses'), may hold values from -2 to 2
Outputs:
- error: bfloat16 [32768, 4096], P(('dp', 'context'), 'ulysses'), parts along dimension 0
- grad_keys: bfloat16 [32768, 512], P(('dp', 'context'), 'ulysses'), parts along dimension 0
- grad_feat_q: float32 [64, 128, 128], P(('dp', 'ulysses')), parts along dimension 0
- grad_feat_k: float32 [8, 128, 128], P(('dp', 'ulysses')), parts along dimension 0
The draws below stay inside these ranges and needn't reach their ends.
There are 2 independent parts, one for each index of `dp`. The reference program is written for one: setup_inputs(seed, part) draws one part's arguments, and reference() takes and returns one part's arrays. A program takes and returns all parts, laid end to end along the dimension named above; an argument that names none is the same for every part. Nothing has to cross between parts.
Inputs may be any that keep to these rules, and one draw needn't show every extreme that they name: `segments`: document numbers never fall along the sequence; each document covers 1 to 4096 positions, and one covers exactly 4096.
All inputs are finite; a program needn't handle non-finite values.
Results may differ from the reference program's by a relative error of at most 0.015.
Values may be sent and summed in bfloat16 or wider, within the bound.
A program may use at most 128 MiB of HBM per device.

```python
import math
import jax
import jax.numpy as jnp
import numpy as np
from jax import lax

H = 32
KVH = 4
E = 128
F = 128
WIN = 128
TOKENS = 16384
DOCS = 64
LONGEST = 4096
N_CONTEXT = 32


channel_mean = 0.3


map_offset = 1.2


map_spread = 1.6


def drawn_field(key, salt, width):
    noise = jax.random.normal(jax.random.fold_in(key, salt), (TOKENS, width), jnp.float32)
    return jnp.clip(noise + channel_mean, -5.0, 5.0)


def draw_queries(key, part):
    field = drawn_field(key, 1, H * E)
    return field.astype(jnp.bfloat16)


def draw_keys(key, part):
    field = drawn_field(key, 2, KVH * E)
    return field.astype(jnp.bfloat16)


def draw_values(key, part):
    field = drawn_field(key, 2, KVH * E)
    noise = jax.random.normal(jax.random.fold_in(key, 3), (TOKENS, KVH * E), jnp.float32)
    centred = (field - channel_mean).reshape(TOKENS, KVH, E)
    order = jax.random.permutation(jax.random.fold_in(key, 7), E)
    flips = jnp.where(jax.random.bernoulli(jax.random.fold_in(key, 8), 0.5, (KVH, E)), 1.0, -1.0)
    mixed = 0.7 * flips[None] * centred[:, :, order] + 0.7 * noise.reshape(TOKENS, KVH, E)
    return jnp.clip(mixed.reshape(TOKENS, KVH * E), -6.0, 6.0).astype(jnp.bfloat16)


def map_field(key, salt, heads):
    raw = jax.random.normal(jax.random.fold_in(key, salt), (heads, E, F), jnp.float32)
    return jnp.clip((map_spread * raw - map_offset) / E ** 0.5, -2.0, 2.0)


def draw_feat_q(key, part):
    field = map_field(key, 11, H)
    return field.astype(jnp.bfloat16)


def draw_feat_k(key, part):
    field = map_field(key, 12, KVH)
    return field.astype(jnp.bfloat16)


def length_profile(number_of, total, most, skew):
    weights = [(1 << 20) // math.isqrt(grade ** skew) + 1 for grade in range(2, number_of + 1)]
    surplus, holding = total - most - (number_of - 1), [1] * (number_of - 1)
    while surplus > 0:
        movable = [i for i in range(number_of - 1) if holding[i] < most]
        pool, left = sum([weights[i] for i in movable]), surplus
        for i in movable:
            addition = min(most - holding[i], max(1, left * weights[i] // pool), surplus)
            holding[i] = holding[i] + addition
            surplus = surplus - addition
    return np.array([most] + holding)


def uneven_parts(key, number_of, total, most, skew):
    if number_of == 2:
        one = jax.random.randint(key, (), max(1, total - most), min(most, total - 1) + 1)
        return jnp.stack([one, total - one])
    lengths = jnp.asarray(length_profile(number_of, total, most, skew), jnp.int32)
    couples = (number_of - 1) // 2
    source_of, receiver = lengths[1:1 + 2 * couples:2], lengths[2:2 + 2 * couples:2]
    room = jnp.minimum(source_of - 1, most - receiver)
    passed = jax.random.randint(jax.random.fold_in(key, 1), (couples,), 0, 1 << 20) % (room + 1)
    lengths = lengths.at[1:1 + 2 * couples:2].set(source_of - passed).at[2:2 + 2 * couples:2].set(receiver + passed)
    return lengths[jax.random.permutation(jax.random.fold_in(key, 2), number_of)]


def setup_inputs(seed: int = 0, part: int = 0) -> dict:
    splits = jax.random.split(jax.random.key(seed), 7)
    part_keys = jax.random.split(jax.random.fold_in(splits[6], part), 7)
    queries = draw_queries(jax.random.fold_in(jax.random.fold_in(splits[6], part), 71), part)
    keys = draw_keys(jax.random.fold_in(jax.random.fold_in(splits[6], part), 71), part)
    values = draw_values(jax.random.fold_in(jax.random.fold_in(splits[6], part), 71), part)
    segments = jnp.searchsorted(jnp.cumsum(uneven_parts(part_keys[3], DOCS, TOKENS, LONGEST, 2)), jnp.arange(TOKENS), side="right").astype(jnp.int32)
    feat_q = draw_feat_q(jax.random.fold_in(splits[6], 71), part)
    feat_k = draw_feat_k(jax.random.fold_in(splits[6], 71), part)
    return {"queries": queries, "keys": keys, "values": values, "segments": segments, "feat_q": feat_q, "feat_k": feat_k}


def feature_map(pre):
    return jnp.where(pre > 0, pre + 1.0, jnp.exp(jnp.minimum(pre, 0.0)))

def feature_slope(pre):
    return jnp.where(pre > 0, 1.0, jnp.exp(jnp.minimum(pre, 0.0)))

def join_parts(earlier, later):
    empty_later = later[2] < 0
    keep = (earlier[2] == later[2]) | empty_later
    return (later[0] + jnp.where(keep, earlier[0], 0.0), later[1] + jnp.where(keep, earlier[1], 0.0), jnp.where(empty_later, earlier[2], later[2]))

def mix(form, left, right):
    return jnp.einsum(form, left.astype(jnp.float32), right.astype(jnp.float32), precision=lax.Precision.HIGHEST)

def reference(queries, keys, values, segments, feat_q, feat_k):
    shards = N_CONTEXT
    length = TOKENS // shards
    group = H // KVH
    q_blocks = queries.reshape(shards, length, KVH, group, E)
    k_blocks = keys.reshape(shards, length, KVH, E)
    v_blocks = values.reshape(shards, length, KVH, E)
    s_blocks = segments.reshape(shards, length)
    feat_grouped = feat_q.reshape(KVH, group, E, F)

    def local_state(item):
        key_rows, value_rows, ids = item
        phi_k = feature_map(mix('rge,gef->rgf', key_rows, feat_k)).astype(jnp.bfloat16)
        last_id = ids[length - 1]
        tail = jnp.where((ids == last_id)[:, None, None], phi_k, jnp.zeros_like(phi_k))
        return (mix('rgf,rge->gfe', tail, value_rows), lax.optimization_barrier(jnp.sum(tail.astype(jnp.float32), axis=0)), last_id)
    states, norms, last_ids = lax.map(local_state, (k_blocks, v_blocks, s_blocks))

    def pass_on(carry, item):
        return (join_parts(carry, item), carry)
    anchor = (jnp.zeros((KVH, F, E), jnp.float32), jnp.zeros((KVH, F), jnp.float32), jnp.int32(-1))
    _, (state_in, norm_in, id_in) = lax.scan(pass_on, anchor, (states, norms, last_ids))
    rim_keys = jnp.concatenate([jnp.zeros((1, WIN, KVH, E), keys.dtype), k_blocks[:-1, length - WIN:]], axis=0)
    rim_values = jnp.concatenate([jnp.zeros((1, WIN, KVH, E), values.dtype), v_blocks[:-1, length - WIN:]], axis=0)
    rim_ids = jnp.concatenate([jnp.full((1, WIN), -1, jnp.int32), s_blocks[:-1, length - WIN:].astype(jnp.int32)], axis=0)
    inv_scale = 1.0 / math.sqrt(E)

    def block_pass(item):
        query_rows, key_rows, value_rows, ids, edge_keys, edge_values, edge_ids, c_state, c_norm, c_id = item
        pre_q = mix('rgke,gkef->rgkf', query_rows, feat_grouped)
        phi_q = feature_map(pre_q).astype(jnp.bfloat16)
        phi_k = feature_map(mix('rge,gef->rgf', key_rows, feat_k)).astype(jnp.bfloat16)
        place = jnp.arange(length)
        linked = (place[None, :] <= place[:, None]) & (ids[None, :] == ids[:, None])
        linked = linked[:, None, None, :]
        score = jnp.where(linked, mix('igkf,jgf->igkj', phi_q, phi_k), 0.0)
        take = (ids == c_id)[:, None, None]
        numer = mix('igkj,jge->igke', score.astype(jnp.bfloat16), value_rows) + jnp.where(take[..., None], mix('igkf,gfe->igke', phi_q, c_state), 0.0)
        denom = lax.optimization_barrier(jnp.sum(score, axis=-1)) + jnp.where(take, mix('igkf,gf->igk', phi_q, c_norm), 0.0)
        student = numer / denom[..., None]
        keys_ext = jnp.concatenate([edge_keys, key_rows], axis=0)
        values_ext = jnp.concatenate([edge_values, value_rows], axis=0)
        ids_ext = jnp.concatenate([edge_ids, ids.astype(jnp.int32)], axis=0)
        place_ext = jnp.arange(length + WIN) - WIN
        seen = (place_ext[None, :] <= place[:, None]) & (place_ext[None, :] > place[:, None] - WIN) & (ids_ext[None, :] == ids[:, None])
        logits = jnp.where(seen[:, None, None, :], mix('igke,jge->igkj', query_rows, keys_ext) * inv_scale, -jnp.inf)
        top = lax.optimization_barrier(jnp.max(logits, axis=-1, keepdims=True))
        probs = jnp.exp(logits - top)
        teacher = mix('igkj,jge->igke', probs.astype(jnp.bfloat16), values_ext) / lax.optimization_barrier(jnp.sum(probs, axis=-1))[..., None]
        gap = student - teacher
        upstream = 32.0 * gap
        d_numer = (upstream / denom[..., None]).astype(jnp.bfloat16)
        d_denom = -lax.optimization_barrier(jnp.sum(upstream * student, axis=-1)) / denom
        d_score = jnp.where(linked, mix('igke,jge->igkj', d_numer, value_rows) + d_denom[..., None], 0.0).astype(jnp.bfloat16)
        d_phi_q = mix('igkj,jgf->igkf', d_score, phi_k) + jnp.where(take[..., None], mix('gfe,igke->igkf', c_state, d_numer) + d_denom[..., None] * c_norm[None, :, None, :], 0.0)
        d_phi_k = mix('igkj,igkf->jgf', d_score, phi_q)
        head_rows = (ids == ids[0])[:, None, None, None]
        phi_head = jnp.where(head_rows, phi_q, jnp.zeros_like(phi_q))
        cot_state = mix('igkf,igke->gfe', phi_head, d_numer)
        cot_norm = lax.optimization_barrier(jnp.sum(jnp.where(head_rows, d_denom[..., None] * phi_q.astype(jnp.float32), 0.0), axis=(0, 2)))
        d_pre_q = (d_phi_q * feature_slope(pre_q)).astype(jnp.bfloat16)
        grad_q = mix('rgke,rgkf->gkef', query_rows, d_pre_q)
        return (gap.astype(jnp.bfloat16), d_phi_k, cot_state, cot_norm, ids[0], grad_q)
    gaps, d_phi_ks, cot_states, cot_norms, first_ids, grad_qs = lax.map(block_pass, (q_blocks, k_blocks, v_blocks, s_blocks, rim_keys, rim_values, rim_ids, state_in, norm_in, id_in))
    _, (back_state, back_norm, back_id) = lax.scan(pass_on, anchor, (cot_states, cot_norms, first_ids), reverse=True)

    def finish(item):
        key_rows, value_rows, ids, d_phi_k, b_state, b_norm, b_id = item
        pre_k = mix('rge,gef->rgf', key_rows, feat_k)
        take = (ids == b_id)[:, None, None]
        d_phi_k = d_phi_k + jnp.where(take, mix('gfe,jge->jgf', b_state, value_rows) + b_norm[None], 0.0)
        d_pre_k = (d_phi_k * feature_slope(pre_k)).astype(jnp.bfloat16)
        key_grad = mix('jgf,gef->jge', d_pre_k, feat_k).astype(jnp.bfloat16)
        return (key_grad, mix('rge,rgf->gef', key_rows, d_pre_k))
    key_grads, grad_ks = lax.map(finish, (k_blocks, v_blocks, s_blocks, d_phi_ks, back_state, back_norm, back_id))
    scale = 1.0 / math.sqrt(TOKENS)
    error = gaps.reshape(TOKENS, H * E)
    grad_keys = key_grads.reshape(TOKENS, KVH * E)
    grad_feat_q = lax.optimization_barrier(jnp.sum(grad_qs, axis=0)).reshape(H, E, F) * scale
    grad_feat_k = lax.optimization_barrier(jnp.sum(grad_ks, axis=0)) * scale
    return (error, grad_keys, grad_feat_q, grad_feat_k)
```

```python
import functools
import math

import jax
import jax.numpy as jnp
from jax import lax
from jax.experimental import pallas as pl
from jax.experimental.pallas import tpu as pltpu
from jax.sharding import PartitionSpec as P

WIN = 128
REACH = 8
TAIL = 16
MESH = pl.DeviceIdType.MESH
F32 = jnp.float32
BF16 = jnp.bfloat16


def dot_nn(a, b):
    return lax.dot_general(a, b, (((1,), (0,)), ((), ())), preferred_element_type=F32)


def dot_nt(a, b):
    return lax.dot_general(a, b, (((1,), (1,)), ((), ())), preferred_element_type=F32)


def dot_tn(a, b):
    return lax.dot_general(a, b, (((0,), (0,)), ((), ())), preferred_element_type=F32)


def remote(src, dst, send, recv, **where):
    return pltpu.make_async_remote_copy(
        src_ref=src, dst_ref=dst, send_sem=send, recv_sem=recv, device_id=where, device_id_type=MESH
    )


def whole(ref, sem):
    return pltpu.make_async_copy(ref, ref, sem)


def columns_of(seg_row):
    length = seg_row.shape[1]
    parts = [
        jnp.transpose(jnp.broadcast_to(seg_row[:, i : i + 128].astype(F32), (128, 128)))
        for i in range(0, length, 128)
    ]
    return jnp.concatenate(parts, axis=0)


def payload(state, norm, ident):
    row = lax.broadcasted_iota(jnp.int32, (TAIL, norm.shape[1]), 0)
    tail = jnp.where(row == 0, norm, jnp.where(row == 1, ident, 0.0))
    return state.astype(BF16), tail.astype(BF16)


def gathered(buf, ident, here, count, forward):
    feats = buf.shape[1] - TAIL
    state = jnp.zeros((feats, buf.shape[2]), F32)
    norm = jnp.zeros((1, buf.shape[2]), F32)
    for k in range(REACH):
        inside = here > k if forward else here + k + 1 < count
        tail = buf[k, feats : feats + TAIL, :].astype(F32)
        keep = (tail[1:2, :] == ident) & inside
        state += jnp.where(keep, buf[k, 0:feats, :].astype(F32), 0.0)
        norm += jnp.where(keep, tail[0:1, :], 0.0)
    return state, norm


def enter_kernel(
    q_ref, k_ref, v_ref, seg_ref, fk_ref,
    q_out, kx_out, vx_out, rim_out, phi_out, slope_out, state_out, norm_out,
    sbuf, rbuf, rim_in, qs, ks, vs, qr, kr, vr, rs, rr, xs, xr,
):
    here, mine = lax.axis_index("context"), lax.axis_index("ulysses")
    count, split = lax.axis_size("context"), lax.axis_size("ulysses")
    rows = k_ref.shape[0]
    wide, thin = q_out.shape[1], kx_out.shape[1]
    length = rows * split

    barrier = pltpu.get_barrier_semaphore()
    for j in range(1, split):
        pl.semaphore_signal(
            barrier, inc=1, device_id={"ulysses": lax.rem(mine + j, split)}, device_id_type=MESH
        )
    for k in range(1, REACH + 1):
        for other in (lax.rem(here + k, count), lax.rem(here + count - k, count)):
            pl.semaphore_signal(barrier, inc=1, device_id={"context": other}, device_id_type=MESH)

    def piece(ref, who, size):
        return ref.at[:, pl.ds(pl.multiple_of(who * size, 128), size)]

    def place(ref, start):
        return ref.at[pl.ds(pl.multiple_of(start + mine * rows, 128), rows), :]

    jobs = (
        (k_ref, kx_out, thin, WIN, ks, kr),
        (v_ref, vx_out, thin, WIN, vs, vr),
        (q_ref, q_out, wide, 0, qs, qr),
    )
    for src, dst, size, start, _, recv in jobs:
        pltpu.make_async_copy(piece(src, mine, size), place(dst, start), recv).start()
    pl.semaphore_wait(barrier, split - 1 + 2 * REACH)

    sends = []
    for src, dst, size, start, send, recv in jobs:
        for j in range(1, split):
            peer = lax.rem(mine + j, split)
            copy = remote(
                piece(src, peer, size), place(dst, start), send.at[j - 1], recv, ulysses=peer
            )
            copy.start()
            sends.append(copy)

    whole(kx_out.at[pl.ds(WIN, length), :], kr).wait()
    whole(vx_out.at[pl.ds(WIN, length), :], vr).wait()
    after = lax.rem(here + 1, count)
    edge = pl.ds(length, WIN)
    rims = [
        remote(kx_out.at[edge, :], kx_out.at[pl.ds(0, WIN), :], rs.at[0], rr.at[0], context=after),
        remote(vx_out.at[edge, :], vx_out.at[pl.ds(0, WIN), :], rs.at[1], rr.at[1], context=after),
        remote(seg_ref.at[:, pl.ds(length - WIN, WIN)], rim_in, rs.at[2], rr.at[2], context=after),
    ]
    for copy in rims:
        copy.start()

    seg_row = seg_ref[...]
    seg_col = columns_of(seg_row)
    last_id = jnp.max(seg_row, axis=1, keepdims=True).astype(F32)
    first_id = jnp.min(seg_row, axis=1, keepdims=True).astype(F32)
    pre = dot_nn(kx_out[WIN : WIN + length, :], fk_ref[...])
    small = jnp.exp(jnp.minimum(pre, 0.0))
    phi = jnp.where(pre > 0, pre + 1.0, small)
    phi_out[...] = phi.astype(BF16)
    slope_out[...] = jnp.where(pre > 0, 1.0, small)
    tail = jnp.where(seg_col == last_id, phi.astype(BF16).astype(F32), 0.0)
    feats = phi.shape[1]
    state, end = payload(
        dot_tn(tail.astype(BF16), vx_out[WIN : WIN + length, :]),
        jnp.sum(tail, axis=0, keepdims=True),
        last_id,
    )
    sbuf[0:feats, :] = state
    sbuf[feats : feats + TAIL, :] = end
    for k in range(REACH):
        copy = remote(sbuf, rbuf.at[k], xs.at[k], xr.at[k], context=lax.rem(here + k + 1, count))
        copy.start()
        sends.append(copy)
    for k in range(REACH):
        whole(rbuf.at[k], xr.at[k]).wait()
    state_in, norm_in = gathered(rbuf, first_id, here, count, True)
    state_out[...] = state_in.astype(BF16)
    norm_out[...] = jnp.broadcast_to(norm_in, norm_out.shape)
    for copy in rims:
        copy.wait()
    rim_out[...] = jnp.where(here > 0, rim_in[...], -1)
    whole(q_out, qr).wait()
    for copy in sends:
        copy.wait_send()


def core_kernel(
    q_ref, kx_ref, vx_ref, rim_ref, seg_ref, fq_ref, phik_ref, state_ref, norm_ref,
    err_ref, gq_ref, dphik_ref, cot_ref,
    mask, bias, take, phi_s, slope_s, dn_s, dd_s, acc,
):
    heads, width, feats = fq_ref.shape
    length = q_ref.shape[0]
    step = 256
    inv_scale = 1.0 / math.sqrt(width)

    seg_row = seg_ref[...]
    first_id = jnp.min(seg_row, axis=1, keepdims=True).astype(F32)
    rows_f = seg_row.astype(F32)
    rim_f = rim_ref[...].astype(F32)
    seg_col = columns_of(seg_row)
    take[...] = jnp.where(seg_col == first_id, 1.0, 0.0)
    r = lax.broadcasted_iota(jnp.int32, (128, 128), 0)
    c = lax.broadcasted_iota(jnp.int32, (128, 128), 1)
    for i in range(0, length, 128):
        col = seg_col[i : i + 128, :]
        for j in range(0, length, 128):
            if j > i:
                mask[i : i + 128, j : j + 128] = jnp.zeros((128, 128), F32)
                continue
            same = col == rows_f[:, j : j + 128]
            if j == i:
                same = same & (c <= r)
            mask[i : i + 128, j : j + 128] = jnp.where(same, 1.0, 0.0)
        before = rim_f if i == 0 else rows_f[:, i - 128 : i]
        bias[i : i + 128, 0:128] = jnp.where((col == before) & (c > r), 0.0, -1e30)
        bias[i : i + 128, 128:256] = jnp.where(
            (col == rows_f[:, i : i + 128]) & (c <= r), 0.0, -1e30
        )

    def lanes(h):
        return pl.ds(pl.multiple_of(h * width, 128), width)

    cot_ref[...] = jnp.zeros_like(cot_ref)
    acc[...] = jnp.zeros_like(acc)
    dphik_ref[...] = jnp.zeros_like(dphik_ref)

    def forward(h, _):
        q = q_ref[:, lanes(h)]
        pre = dot_nn(q, fq_ref[h])
        small = jnp.exp(jnp.minimum(pre, 0.0))
        phi = jnp.where(pre > 0, pre + 1.0, small).astype(BF16)
        slope_s[h] = jnp.where(pre > 0, 1.0, small)
        phi_s[h] = phi
        norm = norm_ref[0:1, :]
        dns, dds = [], []
        for i in range(0, length, step):
            end = i + step
            part = phi[i:end]
            score = dot_nt(part, phik_ref[0:end, :]) * mask[i:end, 0:end]
            own = take[i:end, :]
            numer = dot_nn(score.astype(BF16), vx_ref[WIN : WIN + end, :])
            numer += own * dot_nn(part, state_ref[...])
            denom = jnp.sum(score, axis=1, keepdims=True)
            denom += jnp.sum(own * (part.astype(F32) * norm), axis=1, keepdims=True)
            inv = 1.0 / denom
            student = numer * inv
            teachers = []
            for j in range(i, end, 128):
                logits = dot_nt(q[j : j + 128], kx_ref[j : j + 256, :]) * inv_scale
                logits += bias[j : j + 128, :]
                probs = jnp.exp(logits - jnp.max(logits, axis=1, keepdims=True))
                total = jnp.sum(probs, axis=1, keepdims=True)
                teachers.append(dot_nn(probs.astype(BF16), vx_ref[j : j + 256, :]) / total)
            gap = student - jnp.concatenate(teachers, axis=0)
            err_ref[i:end, lanes(h)] = gap.astype(BF16)
            up = 32.0 * gap
            dn = (up * inv).astype(BF16)
            dd = -jnp.sum(up * student, axis=1, keepdims=True) * inv
            dn_s[h, i:end, :] = dn
            dd_s[h, i:end, :] = dd
            dns.append(dn)
            dds.append(dd)
        lead = phi.astype(F32) * take[...]
        acc[...] += jnp.sum(
            (lead * jnp.concatenate(dds, axis=0)).reshape(length // 8, 8, feats), axis=0
        )
        cot_ref[0:feats, :] += dot_tn(lead.astype(BF16), jnp.concatenate(dns, axis=0))
        return 0

    lax.fori_loop(0, heads, forward, 0)
    last_id = jnp.max(seg_row, axis=1, keepdims=True)
    row = lax.broadcasted_iota(jnp.int32, (TAIL, feats), 0)
    total = jnp.sum(acc[...], axis=0, keepdims=True)
    cot_ref[feats : feats + TAIL, :] = jnp.where(
        row == 0, total, jnp.where(row == 1, first_id, 0.0)
    )

    def backward(h, _):
        q = q_ref[:, lanes(h)]
        norm = norm_ref[0:1, :]
        outs = []
        for i in range(0, length, step):
            end = i + step
            dn = dn_s[h, i:end, :]
            dd = dd_s[h, i:end, :]
            own = take[i:end, :]
            d_score = dot_nt(dn, vx_ref[WIN : WIN + end, :]) + dd
            d_score = (d_score * mask[i:end, 0:end]).astype(BF16)
            d_phi = dot_nn(d_score, phik_ref[0:end, :])
            d_phi += own * (dot_nt(dn, state_ref[...]) + dd * norm)
            dphik_ref[0:end, :] += dot_tn(d_score, phi_s[h, i:end, :])
            outs.append((d_phi * slope_s[h, i:end, :]).astype(BF16))
        gq_ref[h] = dot_tn(q, jnp.concatenate(outs, axis=0)).astype(BF16)
        return 0

    lax.fori_loop(0, heads, backward, 0)
    del last_id


def leave_kernel(
    gq_ref, cot_ref, dphik_ref, slope_ref, kx_ref, vx_ref, fk_ref, seg_ref,
    gq_out, keys_out, gk_out,
    sbuf, rbuf, part, red, spread, kpart, kparts, kred, kspread,
    xs, xr, s1, r1, s2, r2, s3, r3, s4, r4,
):
    here = lax.axis_index("context")
    count = lax.axis_size("context")
    feats, width = cot_ref.shape[0] - TAIL, cot_ref.shape[1]
    length = dphik_ref.shape[0]
    scale = 1.0 / math.sqrt(length * count)

    barrier = pltpu.get_barrier_semaphore()

    def greet(k, _):
        pl.semaphore_signal(
            barrier, inc=1, device_id={"context": lax.rem(here + k, count)}, device_id_type=MESH
        )
        return 0

    lax.fori_loop(1, count, greet, 0)
    sbuf[...] = cot_ref[...].astype(BF16)
    pl.semaphore_wait(barrier, count - 1)

    sends = []
    for k in range(REACH):
        copy = remote(
            sbuf, rbuf.at[k], xs.at[k], xr.at[k], context=lax.rem(here + count - k - 1, count)
        )
        copy.start()
        sends.append(copy)

    pltpu.make_async_copy(gq_ref.at[here], part.at[here], r1).start()

    def scatter(k, _):
        peer = lax.rem(here + k, count)
        remote(gq_ref.at[peer], part.at[here], s1, r1, context=peer).start()
        return 0

    lax.fori_loop(1, count, scatter, 0)

    for k in range(REACH):
        whole(rbuf.at[k], xr.at[k]).wait()
    seg_row = seg_ref[...]
    last_id = jnp.max(seg_row, axis=1, keepdims=True).astype(F32)
    back, back_norm = gathered(rbuf, last_id, here, count, False)
    own = jnp.where(columns_of(seg_row) == last_id, 1.0, 0.0)
    d_phi = dphik_ref[...] + own * (
        dot_nt(vx_ref[WIN : WIN + length, :], back.astype(BF16)) + back_norm
    )
    d_pre = (d_phi * slope_ref[...]).astype(BF16)
    keys_out[...] = dot_nt(d_pre, fk_ref[...]).astype(BF16)
    grad = dot_tn(kx_ref[WIN : WIN + length, :], d_pre)
    share = kpart.shape[0]
    kpart[...] = grad.reshape(share, width // share, feats)

    pltpu.make_async_copy(kpart.at[here // 2], kparts.at[here], r3).start()

    def scatter_k(k, _):
        peer = lax.rem(here + k, count)
        remote(kpart.at[peer // 2], kparts.at[here], s3, r3, context=peer).start()
        return 0

    lax.fori_loop(1, count, scatter_k, 0)

    whole(part, r1).wait()
    red[...] = jnp.sum(part[...].astype(F32), axis=0).astype(BF16)
    pltpu.make_async_copy(red, spread.at[here], r2).start()

    def spread_q(k, _):
        peer = lax.rem(here + k, count)
        remote(red, spread.at[here], s2, r2, context=peer).start()
        return 0

    lax.fori_loop(1, count, spread_q, 0)

    whole(kparts, r3).wait()
    kred[...] = jnp.sum(kparts[...], axis=0)
    pltpu.make_async_copy(kred, kspread.at[here // 2], r4).start()

    def spread_k(k, _):
        peer = lax.rem(here + 2 * k, count)
        remote(kred, kspread.at[here // 2], s4, r4, context=peer).start()
        return 0

    lax.fori_loop(1, count // 2, spread_k, 0)

    whole(spread, r2).wait()
    gq_out[...] = spread[...].astype(F32) * scale
    whole(kspread, r4).wait()
    gk_out[...] = kspread[...] * scale

    for copy in sends:
        copy.wait_send()
    rest = pl.ds(0, count - 1)
    whole(part.at[rest], s1).wait()
    whole(spread.at[rest], s2).wait()
    whole(kparts.at[rest], s3).wait()
    whole(kspread.at[pl.ds(0, count // 2 - 1)], s4).wait()


def on_device(queries, keys, values, segments, feat_q, feat_k):
    rows = keys.shape[0]
    split = lax.axis_size("ulysses")
    count = lax.axis_size("context")
    heads, width, feats = feat_q.shape
    length = rows * split
    seg = segments.reshape(1, length)
    key_map = feat_k.reshape(width, feats)
    shape = jax.ShapeDtypeStruct
    anyway = pl.BlockSpec(memory_space=pl.ANY)
    vmem = pl.BlockSpec(memory_space=pltpu.VMEM)
    dma = pltpu.SemaphoreType.DMA
    ext = length + WIN

    q_all, kx, vx, rim, phi_k, slope_k, state, norm = pl.pallas_call(
        enter_kernel,
        name="enter",
        out_shape=(
            shape((length, heads * width), BF16),
            shape((ext, width), BF16),
            shape((ext, width), BF16),
            shape((1, WIN), jnp.int32),
            shape((length, feats), BF16),
            shape((length, feats), F32),
            shape((feats, width), BF16),
            shape((8, feats), F32),
        ),
        in_specs=[anyway, anyway, anyway, vmem, vmem],
        out_specs=[vmem] * 8,
        scratch_shapes=[
            pltpu.VMEM((feats + TAIL, width), BF16),
            pltpu.VMEM((REACH, feats + TAIL, width), BF16),
            pltpu.VMEM((1, WIN), jnp.int32),
            dma((split - 1,)),
            dma((split - 1,)),
            dma((split - 1,)),
            dma,
            dma,
            dma,
            dma((3,)),
            dma((3,)),
            dma((REACH,)),
            dma((REACH,)),
        ],
        compiler_params=pltpu.CompilerParams(collective_id=0, has_side_effects=True),
    )(queries, keys, values, seg, key_map)

    errors, grad_q, d_phi_k, cot = pl.pallas_call(
        core_kernel,
        name="core",
        out_shape=(
            shape((length, heads * width), BF16),
            shape((heads, width, feats), BF16),
            shape((length, feats), F32),
            shape((feats + TAIL, width), F32),
        ),
        in_specs=[vmem] * 9,
        out_specs=[vmem] * 4,
        scratch_shapes=[
            pltpu.VMEM((length, length), F32),
            pltpu.VMEM((length, 2 * WIN), F32),
            pltpu.VMEM((length, 128), F32),
            pltpu.VMEM((heads, length, feats), BF16),
            pltpu.VMEM((heads, length, feats), F32),
            pltpu.VMEM((heads, length, width), BF16),
            pltpu.VMEM((heads, length, 1), F32),
            pltpu.VMEM((8, feats), F32),
        ],
    )(q_all, kx, vx, rim, seg, feat_q, phi_k, state, norm)

    per = heads * width // count
    share = count // 2
    grad_q, grad_keys, grad_k = pl.pallas_call(
        leave_kernel,
        name="leave",
        out_shape=(
            shape((count, per, feats), F32),
            shape((length, width), BF16),
            shape((share, width // share, feats), F32),
        ),
        in_specs=[vmem] * 8,
        out_specs=[vmem] * 3,
        scratch_shapes=[
            pltpu.VMEM((feats + TAIL, width), BF16),
            pltpu.VMEM((REACH, feats + TAIL, width), BF16),
            pltpu.VMEM((count, per, feats), BF16),
            pltpu.VMEM((per, feats), BF16),
            pltpu.VMEM((count, per, feats), BF16),
            pltpu.VMEM((share, width // share, feats), F32),
            pltpu.VMEM((count, width // share, feats), F32),
            pltpu.VMEM((width // share, feats), F32),
            pltpu.VMEM((share, width // share, feats), F32),
            dma((REACH,)),
            dma((REACH,)),
        ]
        + [dma] * 8,
        compiler_params=pltpu.CompilerParams(collective_id=1, has_side_effects=True),
    )(grad_q.reshape(count, per, feats), cot, d_phi_k, slope_k, kx, vx, key_map, seg)
    return (
        errors,
        grad_keys,
        grad_q.reshape(heads, width, feats),
        grad_k.reshape(feat_k.shape),
    )


def solution(mesh):
    in_specs = (
        P(("dp", "context", "ulysses"), None),
        P(("dp", "context", "ulysses"), None),
        P(("dp", "context", "ulysses"), None),
        P(("dp", "context")),
        P("ulysses", None, None),
        P("ulysses", None, None),
    )
    out_specs = (
        P(("dp", "context"), "ulysses"),
        P(("dp", "context"), "ulysses"),
        P(("dp", "ulysses"), None, None),
        P(("dp", "ulysses"), None, None),
    )
    return jax.shard_map(
        on_device, mesh=mesh, in_specs=in_specs, out_specs=out_specs, check_vma=False
    )
```

```python
import functools
import math

import jax
import jax.numpy as jnp
from jax import lax
from jax.experimental import pallas as pl
from jax.experimental.pallas import tpu as pltpu
from jax.sharding import PartitionSpec as P

WIN = 128
REACH = 8
TAIL = 16
MESH = pl.DeviceIdType.MESH
F32 = jnp.float32
BF16 = jnp.bfloat16


def dot_nn(a, b):
    return lax.dot_general(a, b, (((1,), (0,)), ((), ())), preferred_element_type=F32)


def dot_nt(a, b):
    return lax.dot_general(a, b, (((1,), (1,)), ((), ())), preferred_element_type=F32)


def dot_tn(a, b):
    return lax.dot_general(a, b, (((0,), (0,)), ((), ())), preferred_element_type=F32)


def remote(src, dst, send, recv, **where):
    return pltpu.make_async_remote_copy(
        src_ref=src, dst_ref=dst, send_sem=send, recv_sem=recv, device_id=where, device_id_type=MESH
    )


def whole(ref, sem):
    return pltpu.make_async_copy(ref, ref, sem)


def columns_of(seg_row):
    length = seg_row.shape[1]
    parts = [
        jnp.transpose(jnp.broadcast_to(seg_row[:, i : i + 128].astype(F32), (128, 128)))
        for i in range(0, length, 128)
    ]
    return jnp.concatenate(parts, axis=0)


def payload(state, norm, ident):
    row = lax.broadcasted_iota(jnp.int32, (TAIL, norm.shape[1]), 0)
    tail = jnp.where(row == 0, norm, jnp.where(row == 1, ident, 0.0))
    return state.astype(BF16), tail.astype(BF16)


def gathered(buf, ident, here, count, forward):
    feats = buf.shape[1] - TAIL
    state = jnp.zeros((feats, buf.shape[2]), F32)
    norm = jnp.zeros((1, buf.shape[2]), F32)
    for k in range(REACH):
        inside = here > k if forward else here + k + 1 < count
        tail = buf[k, feats : feats + TAIL, :].astype(F32)
        keep = (tail[1:2, :] == ident) & inside
        state += jnp.where(keep, buf[k, 0:feats, :].astype(F32), 0.0)
        norm += jnp.where(keep, tail[0:1, :], 0.0)
    return state, norm


def step_kernel(
    q_ref, k_ref, v_ref, seg_in, fq_ref, fk_ref,
    err_ref, keys_out, spread, kspread,
    seg_ref, qv, qb, kx, vx, fq, fk, rim_in, sbuf, rbuf, cbuf, dbuf,
    mask, bias, take, lead_s, phi_s, slope_s, num_s, den_s, tea_s, dn_s, dd_s, phik, slopek, dphik, cot, acc,
    gq, part, red, kpart, kparts, kred,
    ql, kl, vl, fl, ks, vs, qs, kr, vr, qr, rs, rr, xs, xr, cs, cr,
    s1, r1, s2, r2, s3, r3, s4, r4,
):
    here, mine = lax.axis_index("context"), lax.axis_index("ulysses")
    count, split = lax.axis_size("context"), lax.axis_size("ulysses")
    rows = k_ref.shape[0]
    heads, width, feats = fq_ref.shape
    length = rows * split
    wide = heads * width
    step = 256
    inv_scale = 1.0 / math.sqrt(width)

    barrier = pltpu.get_barrier_semaphore()
    for j in range(1, split):
        pl.semaphore_signal(
            barrier, inc=1, device_id={"ulysses": lax.rem(mine + j, split)}, device_id_type=MESH
        )

    def greet(k, _):
        pl.semaphore_signal(
            barrier, inc=1, device_id={"context": lax.rem(here + k, count)}, device_id_type=MESH
        )
        return 0

    lax.fori_loop(1, count, greet, 0)

    def place(start):
        return pl.ds(pl.multiple_of(start + mine * rows, 128), rows)

    def lanes(who, size):
        return pl.ds(pl.multiple_of(who * size, 128), size)

    load_seg = pltpu.make_async_copy(seg_in, seg_ref, fl.at[2])
    load_seg.start()
    small = ((k_ref, kx, kl, ks, kr), (v_ref, vx, vl, vs, vr))
    for src, dst, _, _, recv in small:
        pltpu.make_async_copy(src.at[:, lanes(mine, width)], dst.at[place(WIN), :], recv).start()
    load_q = pltpu.make_async_copy(q_ref, qv, ql)
    load_q.start()
    loads = [pltpu.make_async_copy(fq_ref, fq, fl.at[0]), pltpu.make_async_copy(fk_ref, fk, fl.at[1])]
    for copy in loads:
        copy.start()

    load_seg.wait()
    seg_row = seg_ref[...]
    rows_f = seg_row.astype(F32)
    first_id = jnp.min(seg_row, axis=1, keepdims=True).astype(F32)
    last_id = jnp.max(seg_row, axis=1, keepdims=True).astype(F32)
    seg_col = columns_of(seg_row)
    take[...] = jnp.where(seg_col == first_id, 1.0, 0.0)
    r = lax.broadcasted_iota(jnp.int32, (128, 128), 0)
    c = lax.broadcasted_iota(jnp.int32, (128, 128), 1)
    for i in range(0, length, 128):
        col = seg_col[i : i + 128, :]
        for j in range(0, length, 128):
            if j > i:
                mask[i : i + 128, j : j + 128] = jnp.zeros((128, 128), F32)
                continue
            same = col == rows_f[:, j : j + 128]
            if j == i:
                same = same & (c <= r)
            mask[i : i + 128, j : j + 128] = jnp.where(same, 1.0, 0.0)
        if i:
            bias[i : i + 128, 0:128] = jnp.where(
                (col == rows_f[:, i - 128 : i]) & (c > r), 0.0, -1e30
            )
        bias[i : i + 128, 128:256] = jnp.where(
            (col == rows_f[:, i : i + 128]) & (c <= r), 0.0, -1e30
        )
    cot[...] = jnp.zeros_like(cot)
    acc[...] = jnp.zeros_like(acc)
    dphik[...] = jnp.zeros_like(dphik)
    load_q.wait()
    for h in range(heads):
        pltpu.make_async_copy(
            qv.at[:, lanes(mine * heads + h, width)], qb.at[h, place(0), :], qr.at[h]
        ).start()

    pl.semaphore_wait(barrier, split - 1 + count - 1)

    sends = []
    for src, dst, _, send, recv in small:
        for j in range(1, split):
            peer = lax.rem(mine + j, split)
            copy = remote(
                src.at[:, lanes(peer, width)], dst.at[place(WIN), :], send.at[j - 1], recv, ulysses=peer
            )
            copy.start()
            sends.append(copy)

    def send_q(h, _):
        for j in range(1, split):
            peer = lax.rem(mine + j, split)
            remote(
                qv.at[:, lanes(peer * heads + h, width)], qb.at[h, place(0), :], qs, qr.at[h],
                ulysses=peer,
            ).start()
        return 0

    lax.fori_loop(0, heads, send_q, 0)

    for copy in loads:
        copy.wait()
    whole(kx.at[pl.ds(WIN, length), :], kr).wait()
    whole(vx.at[pl.ds(WIN, length), :], vr).wait()
    after = lax.rem(here + 1, count)
    edge, rim = pl.ds(length, WIN), pl.ds(0, WIN)
    rims = [
        remote(kx.at[edge, :], kx.at[rim, :], rs.at[0], rr.at[0], context=after),
        remote(vx.at[edge, :], vx.at[rim, :], rs.at[1], rr.at[1], context=after),
        remote(seg_ref.at[:, pl.ds(length - WIN, WIN)], rim_in, rs.at[2], rr.at[2], context=after),
    ]
    for copy in rims:
        copy.start()

    pre = dot_nn(kx[WIN : WIN + length, :], fk[...])
    low = jnp.exp(jnp.minimum(pre, 0.0))
    phi = jnp.where(pre > 0, pre + 1.0, low).astype(BF16)
    phik[...] = phi
    slopek[...] = jnp.where(pre > 0, 1.0, low)
    tail = jnp.where(seg_col == last_id, phi.astype(F32), 0.0)
    state, end = payload(
        dot_tn(tail.astype(BF16), vx[WIN : WIN + length, :]),
        jnp.sum(tail, axis=0, keepdims=True),
        last_id,
    )
    sbuf[0:feats, :] = state
    sbuf[feats : feats + TAIL, :] = end
    for k in range(REACH):
        copy = remote(sbuf, rbuf.at[k], xs.at[k], xr.at[k], context=lax.rem(here + k + 1, count))
        copy.start()
        sends.append(copy)

    for copy in rims:
        copy.wait()
    rim_f = jnp.where(here > 0, rim_in[...], -1).astype(F32)
    bias[0:128, 0:128] = jnp.where((seg_col[0:128, :] == rim_f) & (c > r), 0.0, -1e30)

    def forward(h, _):
        whole(qb.at[h], qr.at[h]).wait()
        q = qb[h]
        pre = dot_nn(q, fq[h])
        low = jnp.exp(jnp.minimum(pre, 0.0))
        phi = jnp.where(pre > 0, pre + 1.0, low).astype(BF16)
        slope_s[h] = jnp.where(pre > 0, 1.0, low)
        phi_s[h] = phi
        lead_s[h] = (phi.astype(F32) * take[...]).astype(BF16)
        for i in range(0, length, step):
            end = i + step
            score = dot_nt(phi[i:end], phik[0:end, :]) * mask[i:end, 0:end]
            num_s[h, i:end, :] = dot_nn(score.astype(BF16), vx[WIN : WIN + end, :])
            den_s[h, i:end, :] = jnp.sum(score, axis=1, keepdims=True)
            for j in range(i, end, 128):
                logits = dot_nt(q[j : j + 128], kx[j : j + 256, :]) * inv_scale
                logits += bias[j : j + 128, :]
                probs = jnp.exp(logits - jnp.max(logits, axis=1, keepdims=True))
                total = jnp.sum(probs, axis=1, keepdims=True)
                tea_s[h, j : j + 128, :] = dot_nn(probs.astype(BF16), vx[j : j + 256, :]) / total
        return 0

    lax.fori_loop(0, heads, forward, 0)

    for k in range(REACH):
        whole(rbuf.at[k], xr.at[k]).wait()
    state, norm = gathered(rbuf, first_id, here, count, True)
    state = state.astype(BF16)

    def meet(h, _):
        lead = lead_s[h]
        lead_f = lead.astype(F32)
        numer = num_s[h] + dot_nn(lead, state)
        denom = den_s[h] + jnp.sum(lead_f * norm, axis=1, keepdims=True)
        inv = 1.0 / denom
        student = numer * inv
        gap = student - tea_s[h]
        err_ref[:, lanes(h, width)] = gap.astype(BF16)
        up = 32.0 * gap
        dn = (up * inv).astype(BF16)
        dd = -jnp.sum(up * student, axis=1, keepdims=True) * inv
        dn_s[h] = dn
        dd_s[h] = dd
        acc[...] += jnp.sum((lead_f * dd).reshape(length // 8, 8, feats), axis=0)
        cot[...] += dot_tn(lead, dn)
        return 0

    lax.fori_loop(0, heads, meet, 0)
    total, end = payload(cot[...], jnp.sum(acc[...], axis=0, keepdims=True), first_id)
    cbuf[0:feats, :] = total
    cbuf[feats : feats + TAIL, :] = end
    for k in range(REACH):
        copy = remote(
            cbuf, dbuf.at[k], cs.at[k], cr.at[k], context=lax.rem(here + count - k - 1, count)
        )
        copy.start()
        sends.append(copy)

    per = gq.shape[1]
    share = width // per

    def head_of(s):
        return lax.rem(s + here // share, heads)

    def scatter(s):
        for j in range(share):
            owner = head_of(s) * share + j

            @pl.when(owner != here)
            def _():
                remote(gq.at[owner], part.at[here], s1, r1, context=owner).start()

            @pl.when(owner == here)
            def _():
                pltpu.make_async_copy(gq.at[owner], part.at[here], r1).start()

    def backward(s, _):
        h = head_of(s)

        @pl.when(s > 0)
        def _():
            scatter(s - 1)

        outs = []
        for i in range(0, length, step):
            end = i + step
            dn = dn_s[h, i:end, :]
            dd = dd_s[h, i:end, :]
            d_score = dot_nt(dn, vx[WIN : WIN + end, :]) + dd
            d_score = (d_score * mask[i:end, 0:end]).astype(BF16)
            d_phi = dot_nn(d_score, phik[0:end, :])
            d_phi += take[i:end, :] * (dot_nt(dn, state) + dd * norm)
            dphik[0:end, :] += dot_tn(d_score, phi_s[h, i:end, :])
            outs.append((d_phi * slope_s[h, i:end, :]).astype(BF16))
        grad = dot_tn(qb[h], jnp.concatenate(outs, axis=0)).astype(BF16)
        for j in range(share):
            gq[h * share + j] = grad[j * per : (j + 1) * per, :]
        return 0

    lax.fori_loop(0, heads, backward, 0)
    scatter(heads - 1)

    for k in range(REACH):
        whole(dbuf.at[k], cr.at[k]).wait()
    back, back_norm = gathered(dbuf, last_id, here, count, False)
    own = jnp.where(columns_of(seg_ref[...]) == last_id, 1.0, 0.0)
    d_phi = dphik[...] + own * (dot_nt(vx[WIN : WIN + length, :], back.astype(BF16)) + back_norm)
    d_pre = (d_phi * slopek[...]).astype(BF16)
    grad = dot_tn(kx[WIN : WIN + length, :], d_pre)
    kpart[...] = grad.reshape(kpart.shape)

    pltpu.make_async_copy(kpart.at[here // 2], kparts.at[here], r3).start()

    def scatter_k(k, _):
        peer = lax.rem(here + k, count)
        remote(kpart.at[peer // 2], kparts.at[here], s3, r3, context=peer).start()
        return 0

    lax.fori_loop(1, count, scatter_k, 0)
    keys_out[...] = dot_nt(d_pre, fk[...]).astype(BF16)

    whole(part, r1).wait()
    red[...] = jnp.sum(part[...].astype(F32), axis=0).astype(BF16)
    pltpu.make_async_copy(red, spread.at[here], r2).start()

    def spread_q(k, _):
        peer = lax.rem(here + k, count)
        remote(red, spread.at[here], s2, r2, context=peer).start()
        return 0

    lax.fori_loop(1, count, spread_q, 0)

    whole(kparts, r3).wait()
    kred[...] = jnp.sum(kparts[...], axis=0)
    pltpu.make_async_copy(kred, kspread.at[here // 2], r4).start()

    def spread_k(k, _):
        peer = lax.rem(here + 2 * k, count)
        remote(kred, kspread.at[here // 2], s4, r4, context=peer).start()
        return 0

    lax.fori_loop(1, count // 2, spread_k, 0)

    for copy in sends:
        copy.wait_send()
    whole(qb.at[:, pl.ds(0, length - rows), :], qs).wait()
    rest = pl.ds(0, count - 1)
    whole(part.at[rest], s1).wait()
    whole(kparts.at[rest], s3).wait()
    whole(spread.at[rest], s2).wait()
    whole(kspread.at[pl.ds(0, count // 2 - 1)], s4).wait()
    whole(spread, r2).wait()
    whole(kspread, r4).wait()


def store_kernel(scale, err_in, keys_in, gq_in, gk_in, err_out, keys_out, gq_out, gk_out):
    err_out[...] = err_in[...]
    keys_out[...] = keys_in[...]
    gq_out[...] = gq_in[...].astype(F32) * scale
    gk_out[...] = gk_in[...] * scale


def on_device(queries, keys, values, segments, feat_q, feat_k):
    rows = keys.shape[0]
    split = lax.axis_size("ulysses")
    count = lax.axis_size("context")
    heads, width, feats = feat_q.shape
    length = rows * split
    seg = segments.reshape(1, length)
    key_map = feat_k.reshape(width, feats)
    per = heads * width // count
    share = count // 2
    shape = jax.ShapeDtypeStruct
    hbm = pl.BlockSpec(memory_space=pltpu.HBM)
    vmem = pl.BlockSpec(memory_space=pltpu.VMEM)
    dma = pltpu.SemaphoreType.DMA
    stay = functools.partial(pltpu.with_memory_space_constraint, memory_space=pltpu.HBM)
    ext = length + WIN
    packed = feats + TAIL

    outs = pl.pallas_call(
        step_kernel,
        name="step",
        out_shape=(
            shape((length, heads * width), BF16),
            shape((length, width), BF16),
            shape((count, per, feats), BF16),
            shape((share, width // share, feats), F32),
        ),
        in_specs=[hbm] * 6,
        out_specs=[vmem] * 4,
        scratch_shapes=[
            pltpu.VMEM((1, length), jnp.int32),
            pltpu.VMEM((rows, queries.shape[1]), BF16),
            pltpu.VMEM((heads, length, width), BF16),
            pltpu.VMEM((ext, width), BF16),
            pltpu.VMEM((ext, width), BF16),
            pltpu.VMEM((heads, width, feats), BF16),
            pltpu.VMEM((width, feats), BF16),
            pltpu.VMEM((1, WIN), jnp.int32),
            pltpu.VMEM((packed, width), BF16),
            pltpu.VMEM((REACH, packed, width), BF16),
            pltpu.VMEM((packed, width), BF16),
            pltpu.VMEM((REACH, packed, width), BF16),
            pltpu.VMEM((length, length), F32),
            pltpu.VMEM((length, 2 * WIN), F32),
            pltpu.VMEM((length, feats), F32),
            pltpu.VMEM((heads, length, feats), BF16),
            pltpu.VMEM((heads, length, feats), BF16),
            pltpu.VMEM((heads, length, feats), F32),
            pltpu.VMEM((heads, length, width), F32),
            pltpu.VMEM((heads, length, 1), F32),
            pltpu.VMEM((heads, length, width), F32),
            pltpu.VMEM((heads, length, width), BF16),
            pltpu.VMEM((heads, length, 1), F32),
            pltpu.VMEM((length, feats), BF16),
            pltpu.VMEM((length, feats), F32),
            pltpu.VMEM((length, feats), F32),
            pltpu.VMEM((feats, width), F32),
            pltpu.VMEM((8, feats), F32),
            pltpu.VMEM((count, per, feats), BF16),
            pltpu.VMEM((count, per, feats), BF16),
            pltpu.VMEM((per, feats), BF16),
            pltpu.VMEM((share, width // share, feats), F32),
            pltpu.VMEM((count, width // share, feats), F32),
            pltpu.VMEM((width // share, feats), F32),
            dma,
            dma,
            dma,
            dma((3,)),
            dma((split - 1,)),
            dma((split - 1,)),
            dma,
            dma,
            dma,
            dma((heads,)),
            dma((3,)),
            dma((3,)),
            dma((REACH,)),
            dma((REACH,)),
            dma((REACH,)),
            dma((REACH,)),
        ]
        + [dma] * 8,
        compiler_params=pltpu.CompilerParams(
            collective_id=0, has_side_effects=True, vmem_limit_bytes=50 * 1024 * 1024
        ),
    )(stay(queries), stay(keys), stay(values), stay(seg), stay(feat_q), stay(key_map))

    errors, grad_keys, grad_q, grad_k = pl.pallas_call(
        functools.partial(store_kernel, 1.0 / math.sqrt(length * count)),
        name="store",
        out_shape=(
            shape((length, heads * width), BF16),
            shape((length, width), BF16),
            shape((count, per, feats), F32),
            shape((share, width // share, feats), F32),
        ),
        in_specs=[vmem] * 4,
        out_specs=[vmem] * 4,
        compiler_params=pltpu.CompilerParams(vmem_limit_bytes=8 * 1024 * 1024),
    )(*outs)
    return (
        errors,
        grad_keys,
        grad_q.reshape(heads, width, feats),
        grad_k.reshape(feat_k.shape),
    )


def solution(mesh):
    in_specs = (
        P(("dp", "context", "ulysses"), None),
        P(("dp", "context", "ulysses"), None),
        P(("dp", "context", "ulysses"), None),
        P(("dp", "context")),
        P("ulysses", None, None),
        P("ulysses", None, None),
    )
    out_specs = (
        P(("dp", "context"), "ulysses"),
        P(("dp", "context"), "ulysses"),
        P(("dp", "ulysses"), None, None),
        P(("dp", "ulysses"), None, None),
    )
    return jax.shard_map(
        on_device, mesh=mesh, in_specs=in_specs, out_specs=out_specs, check_vma=False
    )
```

```python
import functools
import math

import jax
import jax.numpy as jnp
from jax import lax
from jax.experimental import pallas as pl
from jax.experimental.pallas import tpu as pltpu
from jax.sharding import PartitionSpec as P

WIN = 128
REACH = 8
TAIL = 16
MESH = pl.DeviceIdType.MESH
F32 = jnp.float32
BF16 = jnp.bfloat16


def dot_nn(a, b):
    return lax.dot_general(a, b, (((1,), (0,)), ((), ())), preferred_element_type=F32)


def dot_nt(a, b):
    return lax.dot_general(a, b, (((1,), (1,)), ((), ())), preferred_element_type=F32)


def dot_tn(a, b):
    return lax.dot_general(a, b, (((0,), (0,)), ((), ())), preferred_element_type=F32)


def remote(src, dst, send, recv, **where):
    return pltpu.make_async_remote_copy(
        src_ref=src, dst_ref=dst, send_sem=send, recv_sem=recv, device_id=where, device_id_type=MESH
    )


def whole(ref, sem):
    return pltpu.make_async_copy(ref, ref, sem)


def columns_of(seg_row):
    length = seg_row.shape[1]
    parts = [
        jnp.transpose(jnp.broadcast_to(seg_row[:, i : i + 128].astype(F32), (128, 128)))
        for i in range(0, length, 128)
    ]
    return jnp.concatenate(parts, axis=0)


def payload(state, norm, ident):
    row = lax.broadcasted_iota(jnp.int32, (TAIL, norm.shape[1]), 0)
    tail = jnp.where(row == 0, norm, jnp.where(row == 1, ident, 0.0))
    return state.astype(BF16), tail.astype(BF16)


def gathered(buf, ident, here, count, forward):
    feats = buf.shape[1] - TAIL
    state = jnp.zeros((feats, buf.shape[2]), F32)
    norm = jnp.zeros((1, buf.shape[2]), F32)
    for k in range(REACH):
        inside = here > k if forward else here + k + 1 < count
        tail = buf[k, feats : feats + TAIL, :].astype(F32)
        keep = (tail[1:2, :] == ident) & inside
        state += jnp.where(keep, buf[k, 0:feats, :].astype(F32), 0.0)
        norm += jnp.where(keep, tail[0:1, :], 0.0)
    return state, norm


def step_kernel(
    q_ref, k_ref, v_ref, seg_in, fq_ref, fk_ref,
    err_ref, keys_out, spread, kspread,
    seg_ref, qv, qb, kx, vx, fq, fk, rim_in, sbuf, rbuf, cbuf, dbuf,
    mask, bias, take, lead_s, phi_s, slope_s, num_s, den_s, tea_s, dn_s, dd_s, phik, slopek, dphik, cot, acc,
    gq, xin, zsend, zin, red, kpart, kxin, kmid, kzin, kred,
    ql, kl, vl, fl, ks, vs, qs, kr, vr, qr, rs, rr, xs, xr, cs, cr,
    s1, r1, s2, r2, s3, r3, s4, r4, s5, r5, s6, r6, s7, r7, ra,
):
    here, mine = lax.axis_index("context"), lax.axis_index("ulysses")
    count, split = lax.axis_size("context"), lax.axis_size("ulysses")
    rows = k_ref.shape[0]
    heads, width, feats = fq_ref.shape
    length = rows * split
    wide = heads * width
    step = 256
    inv_scale = 1.0 / math.sqrt(width)

    share = count // heads
    row, col_x = here // share, lax.rem(here, share)
    planes = count // share

    def beside(j):
        return {"context": row * share + lax.rem(col_x + j, share)}

    def along(j):
        return {"context": lax.rem(row + j, planes) * share + col_x}

    barrier = pltpu.get_barrier_semaphore()
    near = [{"ulysses": lax.rem(mine + j, split)} for j in range(1, split)]
    near += [beside(j) for j in range(1, share)]
    near += [along(j) for j in range(1, planes)]
    offsets = [k for k in range(-REACH, REACH + 1) if k]
    near += [{"context": lax.rem(here + k + count, count)} for k in offsets]
    for peer in near:
        pl.semaphore_signal(barrier, inc=1, device_id=peer, device_id_type=MESH)

    def place(start):
        return pl.ds(pl.multiple_of(start + mine * rows, 128), rows)

    def lanes(who, size):
        return pl.ds(pl.multiple_of(who * size, 128), size)

    load_seg = pltpu.make_async_copy(seg_in, seg_ref, fl.at[2])
    load_seg.start()
    small = ((k_ref, kx, kl, ks, kr), (v_ref, vx, vl, vs, vr))
    for src, dst, _, _, recv in small:
        pltpu.make_async_copy(src.at[:, lanes(mine, width)], dst.at[place(WIN), :], recv).start()
    load_q = pltpu.make_async_copy(q_ref, qv, ql)
    load_q.start()
    loads = [pltpu.make_async_copy(fq_ref, fq, fl.at[0]), pltpu.make_async_copy(fk_ref, fk, fl.at[1])]
    for copy in loads:
        copy.start()

    pl.semaphore_wait(barrier, len(near))

    sends = []
    for src, dst, _, send, recv in small:
        for j in range(1, split):
            peer = lax.rem(mine + j, split)
            copy = remote(
                src.at[:, lanes(peer, width)], dst.at[place(WIN), :], send.at[j - 1], recv, ulysses=peer
            )
            copy.start()
            sends.append(copy)

    load_q.wait()
    for h in range(heads):
        pltpu.make_async_copy(
            qv.at[:, lanes(mine * heads + h, width)], qb.at[h, place(0), :], qr.at[h]
        ).start()

    def send_q(h, _):
        for j in range(1, split):
            peer = lax.rem(mine + j, split)
            remote(
                qv.at[:, lanes(peer * heads + h, width)], qb.at[h, place(0), :], qs, qr.at[h],
                ulysses=peer,
            ).start()
        return 0

    lax.fori_loop(0, heads, send_q, 0)

    load_seg.wait()
    seg_row = seg_ref[...]
    rows_f = seg_row.astype(F32)
    first_id = jnp.min(seg_row, axis=1, keepdims=True).astype(F32)
    last_id = jnp.max(seg_row, axis=1, keepdims=True).astype(F32)
    seg_col = columns_of(seg_row)
    take[...] = jnp.where(seg_col == first_id, 1.0, 0.0)
    r = lax.broadcasted_iota(jnp.int32, (128, 128), 0)
    c = lax.broadcasted_iota(jnp.int32, (128, 128), 1)
    for i in range(0, length, 128):
        col = seg_col[i : i + 128, :]
        for j in range(0, length, 128):
            if j > i:
                mask[i : i + 128, j : j + 128] = jnp.zeros((128, 128), F32)
                continue
            same = col == rows_f[:, j : j + 128]
            if j == i:
                same = same & (c <= r)
            mask[i : i + 128, j : j + 128] = jnp.where(same, 1.0, 0.0)
        if i:
            bias[i : i + 128, 0:128] = jnp.where(
                (col == rows_f[:, i - 128 : i]) & (c > r), 0.0, -1e30
            )
        bias[i : i + 128, 128:256] = jnp.where(
            (col == rows_f[:, i : i + 128]) & (c <= r), 0.0, -1e30
        )
    cot[...] = jnp.zeros_like(cot)
    acc[...] = jnp.zeros_like(acc)
    dphik[...] = jnp.zeros_like(dphik)
    for copy in loads:
        copy.wait()
    whole(kx.at[pl.ds(WIN, length), :], kr).wait()
    whole(vx.at[pl.ds(WIN, length), :], vr).wait()
    after = lax.rem(here + 1, count)
    edge, rim = pl.ds(length, WIN), pl.ds(0, WIN)
    rims = [
        remote(kx.at[edge, :], kx.at[rim, :], rs.at[0], rr.at[0], context=after),
        remote(vx.at[edge, :], vx.at[rim, :], rs.at[1], rr.at[1], context=after),
        remote(seg_ref.at[:, pl.ds(length - WIN, WIN)], rim_in, rs.at[2], rr.at[2], context=after),
    ]
    for copy in rims:
        copy.start()

    pre = dot_nn(kx[WIN : WIN + length, :], fk[...])
    low = jnp.exp(jnp.minimum(pre, 0.0))
    phi = jnp.where(pre > 0, pre + 1.0, low).astype(BF16)
    phik[...] = phi
    slopek[...] = jnp.where(pre > 0, 1.0, low)
    tail = jnp.where(seg_col == last_id, phi.astype(F32), 0.0)
    state, end = payload(
        dot_tn(tail.astype(BF16), vx[WIN : WIN + length, :]),
        jnp.sum(tail, axis=0, keepdims=True),
        last_id,
    )
    sbuf[0:feats, :] = state
    sbuf[feats : feats + TAIL, :] = end
    for k in range(REACH):
        copy = remote(sbuf, rbuf.at[k], xs.at[k], xr.at[k], context=lax.rem(here + k + 1, count))
        copy.start()
        sends.append(copy)

    for copy in rims:
        copy.wait()
    rim_f = jnp.where(here > 0, rim_in[...], -1).astype(F32)
    bias[0:128, 0:128] = jnp.where((seg_col[0:128, :] == rim_f) & (c > r), 0.0, -1e30)

    def forward(h, _):
        whole(qb.at[h], qr.at[h]).wait()
        q = qb[h]
        pre = dot_nn(q, fq[h])
        low = jnp.exp(jnp.minimum(pre, 0.0))
        phi = jnp.where(pre > 0, pre + 1.0, low).astype(BF16)
        slope_s[h] = jnp.where(pre > 0, 1.0, low)
        phi_s[h] = phi
        lead_s[h] = (phi.astype(F32) * take[...]).astype(BF16)
        for i in range(0, length, step):
            end = i + step
            score = dot_nt(phi[i:end], phik[0:end, :]) * mask[i:end, 0:end]
            num_s[h, i:end, :] = dot_nn(score.astype(BF16), vx[WIN : WIN + end, :])
            den_s[h, i:end, :] = jnp.sum(score, axis=1, keepdims=True)
            for j in range(i, end, 128):
                logits = dot_nt(q[j : j + 128], kx[j : j + 256, :]) * inv_scale
                logits += bias[j : j + 128, :]
                probs = jnp.exp(logits - jnp.max(logits, axis=1, keepdims=True))
                total = jnp.sum(probs, axis=1, keepdims=True)
                tea_s[h, j : j + 128, :] = dot_nn(probs.astype(BF16), vx[j : j + 256, :]) / total
        return 0

    lax.fori_loop(0, heads, forward, 0)

    for k in range(REACH):
        whole(rbuf.at[k], xr.at[k]).wait()
    state, norm = gathered(rbuf, first_id, here, count, True)
    state = state.astype(BF16)

    def meet(h, _):
        lead = lead_s[h]
        lead_f = lead.astype(F32)
        numer = num_s[h] + dot_nn(lead, state)
        denom = den_s[h] + jnp.sum(lead_f * norm, axis=1, keepdims=True)
        inv = 1.0 / denom
        student = numer * inv
        gap = student - tea_s[h]
        err_ref[:, lanes(h, width)] = gap.astype(BF16)
        up = 32.0 * gap
        dn = (up * inv).astype(BF16)
        dd = -jnp.sum(up * student, axis=1, keepdims=True) * inv
        dn_s[h] = dn
        dd_s[h] = dd
        acc[...] += jnp.sum((lead_f * dd).reshape(length // 8, 8, feats), axis=0)
        cot[...] += dot_tn(lead, dn)
        return 0

    lax.fori_loop(0, heads, meet, 0)
    total, end = payload(cot[...], jnp.sum(acc[...], axis=0, keepdims=True), first_id)
    cbuf[0:feats, :] = total
    cbuf[feats : feats + TAIL, :] = end
    for k in range(REACH):
        copy = remote(
            cbuf, dbuf.at[k], cs.at[k], cr.at[k], context=lax.rem(here + count - k - 1, count)
        )
        copy.start()
        sends.append(copy)

    per = gq.shape[1]

    def scatter(h):
        pltpu.make_async_copy(gq.at[h * share + col_x], xin.at[col_x, h], r1).start()
        for j in range(1, share):
            to = h * share + lax.rem(col_x + j, share)
            peer = beside(j)
            pltpu.make_async_remote_copy(
                src_ref=gq.at[to], dst_ref=xin.at[col_x, h], send_sem=s1, recv_sem=r1,
                device_id=peer, device_id_type=MESH,
            ).start()

    def backward(h, _):
        @pl.when(h > 0)
        def _():
            scatter(h - 1)

        outs = []
        for i in range(0, length, step):
            end = i + step
            dn = dn_s[h, i:end, :]
            dd = dd_s[h, i:end, :]
            d_score = dot_nt(dn, vx[WIN : WIN + end, :]) + dd
            d_score = (d_score * mask[i:end, 0:end]).astype(BF16)
            d_phi = dot_nn(d_score, phik[0:end, :])
            d_phi += take[i:end, :] * (dot_nt(dn, state) + dd * norm)
            dphik[0:end, :] += dot_tn(d_score, phi_s[h, i:end, :])
            outs.append((d_phi * slope_s[h, i:end, :]).astype(BF16))
        grad = dot_tn(qb[h], jnp.concatenate(outs, axis=0)).astype(BF16)
        for j in range(share):
            gq[h * share + j] = grad[j * per : (j + 1) * per, :]
        return 0

    lax.fori_loop(0, heads, backward, 0)
    scatter(heads - 1)

    for k in range(REACH):
        whole(dbuf.at[k], cr.at[k]).wait()
    back, back_norm = gathered(dbuf, last_id, here, count, False)
    own = jnp.where(columns_of(seg_ref[...]) == last_id, 1.0, 0.0)
    d_phi = dphik[...] + own * (dot_nt(vx[WIN : WIN + length, :], back.astype(BF16)) + back_norm)
    d_pre = (d_phi * slopek[...]).astype(BF16)
    grad = dot_tn(kx[WIN : WIN + length, :], d_pre)
    kpart[...] = grad.reshape(kpart.shape).astype(BF16)

    def send(src, dst, send_sem, recv_sem, peer):
        pltpu.make_async_remote_copy(
            src_ref=src, dst_ref=dst, send_sem=send_sem, recv_sem=recv_sem,
            device_id=peer, device_id_type=MESH,
        ).start()

    def piece(ref, peer):
        return ref.at[lax.rem(peer["context"], share)]

    pltpu.make_async_copy(kpart.at[col_x], kxin.at[col_x], r4).start()
    for j in range(1, share):
        send(piece(kpart, beside(j)), kxin.at[col_x], s4, r4, beside(j))
    keys_out[...] = dot_nt(d_pre, fk[...]).astype(BF16)

    whole(xin, r1).wait()
    zsend[...] = jnp.sum(xin[...].astype(F32), axis=0).astype(BF16)
    pltpu.make_async_copy(zsend.at[row], zin.at[row], r2).start()
    for j in range(1, planes):
        send(zsend.at[lax.rem(row + j, planes)], zin.at[row], s2, r2, along(j))

    whole(kxin, r4).wait()
    kmid[...] = jnp.sum(kxin[...].astype(F32), axis=0).astype(BF16)
    pltpu.make_async_copy(kmid, kzin.at[row], r5).start()
    for j in range(1, planes):
        send(kmid, kzin.at[row], s5, r5, along(j))

    whole(zin, r2).wait()
    red[...] = jnp.sum(zin[...].astype(F32), axis=0).astype(BF16)
    pltpu.make_async_copy(red, spread.at[here], r3).start()
    for j in range(1, planes):
        send(red, spread.at[here], s3, ra.at[row], along(j))
    for j in range(1, share):
        send(red, spread.at[here], s7, r7, beside(j))

    def pass_on(off):
        source = lax.rem(row + off, planes)
        chunk = spread.at[source * share + col_x]
        whole(chunk, ra.at[source]).wait()
        for j in range(1, share):
            send(chunk, chunk, s7, r7, beside(j))

    order = sorted(range(1, planes), key=lambda o: min(o, planes - o))
    for off in order[:-3]:
        pass_on(off)
    whole(kzin, r5).wait()
    kred[...] = jnp.sum(kzin[...].astype(F32), axis=0).astype(BF16)
    pltpu.make_async_copy(kred, kspread.at[col_x], r6).start()
    for j in range(1, share):
        send(kred, kspread.at[col_x], s6, r6, beside(j))
    for off in order[-3:]:
        pass_on(off)

    for copy in sends:
        copy.wait_send()
    whole(qb.at[:, pl.ds(0, length - rows), :], qs).wait()
    whole(xin.at[pl.ds(0, share - 1)], s1).wait()
    whole(zin.at[pl.ds(0, planes - 1)], s2).wait()
    whole(spread.at[pl.ds(0, planes - 1)], s3).wait()
    whole(kxin.at[pl.ds(0, share - 1)], s4).wait()
    whole(kzin.at[pl.ds(0, planes - 1)], s5).wait()
    whole(kspread.at[pl.ds(0, share - 1)], s6).wait()
    beyond = spread.at[pl.ds(0, (share - 1) * planes)]
    whole(beyond, s7).wait()
    whole(spread.at[here], r3).wait()
    whole(kspread, r6).wait()
    whole(beyond, r7).wait()


def store_kernel(scale, err_in, keys_in, gq_in, gk_in, err_out, keys_out, gq_out, gk_out):
    err_out[...] = err_in[...]
    keys_out[...] = keys_in[...]
    gq_out[...] = gq_in[...].astype(F32) * scale
    gk_out[...] = gk_in[...].astype(F32) * scale


def on_device(queries, keys, values, segments, feat_q, feat_k):
    rows = keys.shape[0]
    split = lax.axis_size("ulysses")
    count = lax.axis_size("context")
    heads, width, feats = feat_q.shape
    length = rows * split
    seg = segments.reshape(1, length)
    key_map = feat_k.reshape(width, feats)
    per = heads * width // count
    share = count // heads
    planes = count // share
    shape = jax.ShapeDtypeStruct
    hbm = pl.BlockSpec(memory_space=pltpu.HBM)
    vmem = pl.BlockSpec(memory_space=pltpu.VMEM)
    dma = pltpu.SemaphoreType.DMA
    stay = functools.partial(pltpu.with_memory_space_constraint, memory_space=pltpu.HBM)
    ext = length + WIN
    packed = feats + TAIL

    outs = pl.pallas_call(
        step_kernel,
        name="step",
        out_shape=(
            shape((length, heads * width), BF16),
            shape((length, width), BF16),
            shape((count, per, feats), BF16),
            shape((share, width // share, feats), BF16),
        ),
        in_specs=[hbm] * 6,
        out_specs=[vmem] * 4,
        scratch_shapes=[
            pltpu.VMEM((1, length), jnp.int32),
            pltpu.VMEM((rows, queries.shape[1]), BF16),
            pltpu.VMEM((heads, length, width), BF16),
            pltpu.VMEM((ext, width), BF16),
            pltpu.VMEM((ext, width), BF16),
            pltpu.VMEM((heads, width, feats), BF16),
            pltpu.VMEM((width, feats), BF16),
            pltpu.VMEM((1, WIN), jnp.int32),
            pltpu.VMEM((packed, width), BF16),
            pltpu.VMEM((REACH, packed, width), BF16),
            pltpu.VMEM((packed, width), BF16),
            pltpu.VMEM((REACH, packed, width), BF16),
            pltpu.VMEM((length, length), F32),
            pltpu.VMEM((length, 2 * WIN), F32),
            pltpu.VMEM((length, feats), F32),
            pltpu.VMEM((heads, length, feats), BF16),
            pltpu.VMEM((heads, length, feats), BF16),
            pltpu.VMEM((heads, length, feats), F32),
            pltpu.VMEM((heads, length, width), F32),
            pltpu.VMEM((heads, length, 1), F32),
            pltpu.VMEM((heads, length, width), F32),
            pltpu.VMEM((heads, length, width), BF16),
            pltpu.VMEM((heads, length, 1), F32),
            pltpu.VMEM((length, feats), BF16),
            pltpu.VMEM((length, feats), F32),
            pltpu.VMEM((length, feats), F32),
            pltpu.VMEM((feats, width), F32),
            pltpu.VMEM((8, feats), F32),
            pltpu.VMEM((count, per, feats), BF16),
            pltpu.VMEM((share, planes, per, feats), BF16),
            pltpu.VMEM((planes, per, feats), BF16),
            pltpu.VMEM((planes, per, feats), BF16),
            pltpu.VMEM((per, feats), BF16),
            pltpu.VMEM((share, per, feats), BF16),
            pltpu.VMEM((share, per, feats), BF16),
            pltpu.VMEM((per, feats), BF16),
            pltpu.VMEM((planes, per, feats), BF16),
            pltpu.VMEM((per, feats), BF16),
            dma,
            dma,
            dma,
            dma((3,)),
            dma((split - 1,)),
            dma((split - 1,)),
            dma,
            dma,
            dma,
            dma((heads,)),
            dma((3,)),
            dma((3,)),
            dma((REACH,)),
            dma((REACH,)),
            dma((REACH,)),
            dma((REACH,)),
        ]
        + [dma] * 14
        + [dma((planes,))],
        compiler_params=pltpu.CompilerParams(
            collective_id=0, has_side_effects=True, vmem_limit_bytes=50 * 1024 * 1024
        ),
    )(stay(queries), stay(keys), stay(values), stay(seg), stay(feat_q), stay(key_map))

    errors, grad_keys, grad_q, grad_k = pl.pallas_call(
        functools.partial(store_kernel, 1.0 / math.sqrt(length * count)),
        name="store",
        out_shape=(
            shape((length, heads * width), BF16),
            shape((length, width), BF16),
            shape((count, per, feats), F32),
            shape((share, width // share, feats), F32),
        ),
        in_specs=[vmem] * 4,
        out_specs=[vmem] * 4,
        compiler_params=pltpu.CompilerParams(vmem_limit_bytes=8 * 1024 * 1024),
    )(*outs)
    return (
        errors,
        grad_keys,
        grad_q.reshape(heads, width, feats),
        grad_k.reshape(feat_k.shape),
    )


def solution(mesh):
    in_specs = (
        P(("dp", "context", "ulysses"), None),
        P(("dp", "context", "ulysses"), None),
        P(("dp", "context", "ulysses"), None),
        P(("dp", "context")),
        P("ulysses", None, None),
        P("ulysses", None, None),
    )
    out_specs = (
        P(("dp", "context"), "ulysses"),
        P(("dp", "context"), "ulysses"),
        P(("dp", "ulysses"), None, None),
        P(("dp", "ulysses"), None, None),
    )
    return jax.shard_map(
        on_device, mesh=mesh, in_specs=in_specs, out_specs=out_specs, check_vma=False
    )
```

```python
import functools
import math

import jax
import jax.numpy as jnp
from jax import lax
from jax.experimental import pallas as pl
from jax.experimental.pallas import tpu as pltpu
from jax.sharding import PartitionSpec as P

WIN = 128
REACH = 8
SPLIT = 4
TAIL = 16
MESH = pl.DeviceIdType.MESH
F32 = jnp.float32
BF16 = jnp.bfloat16


def dot_nn(a, b):
    return lax.dot_general(a, b, (((1,), (0,)), ((), ())), preferred_element_type=F32)


def dot_nt(a, b):
    return lax.dot_general(a, b, (((1,), (1,)), ((), ())), preferred_element_type=F32)


def dot_tn(a, b):
    return lax.dot_general(a, b, (((0,), (0,)), ((), ())), preferred_element_type=F32)


def remote(src, dst, send, recv, **where):
    return pltpu.make_async_remote_copy(
        src_ref=src, dst_ref=dst, send_sem=send, recv_sem=recv, device_id=where, device_id_type=MESH
    )


def whole(ref, sem):
    return pltpu.make_async_copy(ref, ref, sem)


def columns_of(seg_row):
    length = seg_row.shape[1]
    parts = [
        jnp.transpose(jnp.broadcast_to(seg_row[:, i : i + 128].astype(F32), (128, 128)))
        for i in range(0, length, 128)
    ]
    return jnp.concatenate(parts, axis=0)


def payload(state, norm, ident):
    row = lax.broadcasted_iota(jnp.int32, (TAIL, norm.shape[1]), 0)
    tail = jnp.where(row == 0, norm, jnp.where(row == 1, ident, 0.0))
    return state.astype(BF16), tail.astype(BF16)


def gathered(buf, ident, here, count, forward):
    feats = buf.shape[1] - TAIL
    state = jnp.zeros((feats, buf.shape[2]), F32)
    norm = jnp.zeros((1, buf.shape[2]), F32)
    for k in range(REACH):
        inside = here > k if forward else here + k + 1 < count
        tail = buf[k, feats : feats + TAIL, :].astype(F32)
        keep = (tail[1:2, :] == ident) & inside
        state += jnp.where(keep, buf[k, 0:feats, :].astype(F32), 0.0)
        norm += jnp.where(keep, tail[0:1, :], 0.0)
    return state, norm


def step_kernel(
    q_ref, k_ref, v_ref, seg_in, fq_ref, fk_ref,
    err_ref, keys_out, spread, kspread,
    seg_ref, qv, qb, kx, vx, fq, fk, rim_in, sbuf, rbuf, cbuf, dbuf, tbuf, ebuf, back_s, backn_s,
    mask, bias, take, takeb, lead_s, phi_s, slope_s, num_s, den_s, tea_s, dn_s, dd_s, phik, slopek, dphik, cot, acc,
    gq, xin, zsend, zin, red, kpart, kxin, kmid, kzin, kred,
    ql, fl, ks, vs, qs, kr, vr, qr, rs, rr, xs, xr, cs, cr, es, er,
    s1, r1, s2, r2, s3, r3, s4, r4, s5, r5, s6, r6, s7, r7, ra,
):
    here, mine = lax.axis_index("context"), lax.axis_index("ulysses")
    count, split = lax.axis_size("context"), lax.axis_size("ulysses")
    rows = k_ref.shape[0]
    heads, width, feats = fq_ref.shape
    length = rows * split
    wide = heads * width
    step = 256
    inv_scale = 1.0 / math.sqrt(width)

    share = count // heads
    row, col_x = here // share, lax.rem(here, share)
    planes = count // share

    def beside(j):
        return {"context": row * share + lax.rem(col_x + j, share)}

    def along(j):
        return {"context": lax.rem(row + j, planes) * share + col_x}

    barrier = pltpu.get_barrier_semaphore()
    near = [{"ulysses": lax.rem(mine + j, split)} for j in range(1, split)]
    near += [beside(j) for j in range(1, share)]
    near += [along(j) for j in range(1, planes)]
    offsets = [k for k in range(-REACH, REACH + 1) if k]
    near += [{"context": lax.rem(here + k + count, count)} for k in offsets]
    for peer in near:
        pl.semaphore_signal(barrier, inc=1, device_id=peer, device_id_type=MESH)

    def place(start):
        return pl.ds(pl.multiple_of(start + mine * rows, 128), rows)

    def lanes(who, size):
        return pl.ds(pl.multiple_of(who * size, 128), size)

    load_seg = pltpu.make_async_copy(seg_in, seg_ref, fl.at[2])
    load_seg.start()
    front = pl.ds(0, width)
    small = ((k_ref, kx, ks, kr), (v_ref, vx, vs, vr))
    for src, dst, _, recv in small:
        pltpu.make_async_copy(
            src.at[:, lanes(mine, width)], dst.at[place(WIN), front], recv.at[mine]
        ).start()
    load_q = pltpu.make_async_copy(q_ref, qv, ql)
    load_q.start()
    loads = [pltpu.make_async_copy(fq_ref, fq, fl.at[0]), pltpu.make_async_copy(fk_ref, fk, fl.at[1])]
    for copy in loads:
        copy.start()

    pl.semaphore_wait(barrier, len(near))

    sends = []
    for src, dst, send, recv in small:
        for j in range(1, split):
            peer = lax.rem(mine + j, split)
            copy = remote(
                src.at[:, lanes(peer, width)], dst.at[place(WIN), front], send.at[j - 1],
                recv.at[mine], ulysses=peer,
            )
            copy.start()
            sends.append(copy)

    load_q.wait()
    for h in range(heads):
        pltpu.make_async_copy(
            qv.at[:, lanes(mine * heads + h, width)], qb.at[h, place(0), :], qr.at[h]
        ).start()

    def send_q(h, _):
        for j in range(1, split):
            peer = lax.rem(mine + j, split)
            remote(
                qv.at[:, lanes(peer * heads + h, width)], qb.at[h, place(0), :], qs, qr.at[h],
                ulysses=peer,
            ).start()
        return 0

    lax.fori_loop(0, heads, send_q, 0)

    load_seg.wait()
    seg_row = seg_ref[...]
    rows_f = seg_row.astype(F32)
    first_id = jnp.min(seg_row, axis=1, keepdims=True).astype(F32)
    last_id = jnp.max(seg_row, axis=1, keepdims=True).astype(F32)
    seg_col = columns_of(seg_row)
    take[...] = jnp.where(seg_col == first_id, 1.0, 0.0)
    takeb[...] = jnp.where(seg_col == first_id, 1.0, 0.0).astype(BF16)
    r = lax.broadcasted_iota(jnp.int32, (128, 128), 0)
    c = lax.broadcasted_iota(jnp.int32, (128, 128), 1)
    for i in range(0, length, 128):
        col = seg_col[i : i + 128, :]
        for j in range(0, length, 128):
            if j > i:
                mask[i : i + 128, j : j + 128] = jnp.zeros((128, 128), F32)
                continue
            same = col == rows_f[:, j : j + 128]
            if j == i:
                same = same & (c <= r)
            mask[i : i + 128, j : j + 128] = jnp.where(same, 1.0, 0.0)
        if i:
            bias[i : i + 128, 0:128] = jnp.where(
                (col == rows_f[:, i - 128 : i]) & (c > r), 0.0, -1e30
            )
        bias[i : i + 128, 128:256] = jnp.where(
            (col == rows_f[:, i : i + 128]) & (c <= r), 0.0, -1e30
        )
    cot[...] = jnp.zeros_like(cot)
    acc[...] = jnp.zeros_like(acc)
    dphik[...] = jnp.zeros_like(dphik)
    for copy in loads:
        copy.wait()
    after = lax.rem(here + 1, count)
    edge, rim = pl.ds(length, WIN), pl.ds(0, WIN)
    rims = [
        remote(seg_ref.at[:, pl.ds(length - WIN, WIN)], rim_in, rs.at[2], rr.at[2], context=after),
        remote(kx.at[edge, front], kx.at[rim, front], rs.at[0], rr.at[0], context=after),
        remote(vx.at[edge, front], vx.at[rim, front], rs.at[1], rr.at[1], context=after),
    ]
    rims[0].start()

    def arrived(ref, sems, who):
        whole(ref.at[pl.ds(WIN + who * rows, rows), front], sems.at[who]).wait()

    arrived(kx, kr, split - 1)
    rims[1].start()
    arrived(vx, vr, split - 1)
    rims[2].start()
    for who in range(split - 1):
        arrived(kx, kr, who)
    for who in range(split - 1):
        arrived(vx, vr, who)

    pre = dot_nn(kx[WIN : WIN + length, :], fk[...])
    low = jnp.exp(jnp.minimum(pre, 0.0))
    phi = jnp.where(pre > 0, pre + 1.0, low).astype(BF16)
    phik[...] = phi
    slopek[...] = jnp.where(pre > 0, 1.0, low)
    tail = jnp.where(seg_col == last_id, phi.astype(F32), 0.0)
    state, end = payload(
        dot_tn(tail.astype(BF16), vx[WIN : WIN + length, 0:width]),
        jnp.sum(tail, axis=0, keepdims=True),
        last_id,
    )
    sbuf[0:feats, :] = state
    sbuf[feats : feats + TAIL, :] = end
    for k in range(REACH):
        copy = remote(sbuf, rbuf.at[k], xs.at[k], xr.at[k], context=lax.rem(here + k + 1, count))
        copy.start()
        sends.append(copy)

    for copy in rims:
        copy.wait()
    rim_f = jnp.where(here > 0, rim_in[...], -1).astype(F32)
    bias[0:128, 0:128] = jnp.where((seg_col[0:128, :] == rim_f) & (c > r), 0.0, -1e30)

    def forward(h, _):
        whole(qb.at[h], qr.at[h]).wait()
        q = qb[h]
        pre = dot_nn(q, fq[h])
        low = jnp.exp(jnp.minimum(pre, 0.0))
        phi = jnp.where(pre > 0, pre + 1.0, low).astype(BF16)
        slope_s[h] = jnp.where(pre > 0, 1.0, low)
        phi_s[h] = phi
        lead_s[h] = phi * takeb[...]
        for i in range(0, length, step):
            end = i + step
            score = dot_nt(phi[i:end], phik[0:end, :]) * mask[i:end, 0:end]
            num_s[h, i:end, :] = dot_nn(score.astype(BF16), vx[WIN : WIN + end, :])
            den_s[h, i:end, :] = jnp.sum(score, axis=1, keepdims=True)
            for j in range(i, end, 128):
                logits = dot_nt(q[j : j + 128], kx[j : j + 256, :]) * inv_scale
                logits += bias[j : j + 128, :]
                probs = jnp.exp(logits - jnp.max(logits, axis=1, keepdims=True))
                total = jnp.sum(probs, axis=1, keepdims=True)
                tea_s[h, j : j + 128, :] = dot_nn(probs.astype(BF16), vx[j : j + 256, :]) * (
                    1.0 / total
                )
        return 0

    lax.fori_loop(0, heads, forward, 0)

    for k in range(REACH):
        whole(rbuf.at[k], xr.at[k]).wait()
    state, norm = gathered(rbuf, first_id, here, count, True)
    state = state.astype(BF16)

    def meet(h, _):
        lead = lead_s[h]
        lead_f = lead.astype(F32)
        inv = 1.0 / (den_s[h] + jnp.sum(lead_f * norm, axis=1, keepdims=True))
        student = (num_s[h] + dot_nn(lead, state)) * inv
        gap = student - tea_s[h]
        err_ref[:, lanes(h, width)] = gap.astype(BF16)
        up = 32.0 * gap
        dn = (up * inv).astype(BF16)
        dd = -jnp.sum(up * student, axis=1, keepdims=True) * inv
        dn_s[h] = dn
        dd_s[h] = dd
        acc[...] += jnp.sum((lead_f * dd).reshape(length // 8, 8, feats), axis=0)
        cot[...] += dot_tn(lead, dn)
        return 0

    def meet_two(t, _):
        meet(2 * t, 0)
        return meet(2 * t + 1, 0)

    lax.fori_loop(0, heads // 2, meet_two, 0)
    total, end = payload(cot[...], jnp.sum(acc[...], axis=0, keepdims=True), first_id)
    cbuf[0:feats, :] = total
    cbuf[feats : feats + TAIL, :] = end

    def send(src, dst, send_sem, recv_sem, peer):
        pltpu.make_async_remote_copy(
            src_ref=src, dst_ref=dst, send_sem=send_sem, recv_sem=recv_sem,
            device_id=peer, device_id_type=MESH,
        ).start()

    for j in range(1, share):
        send(cbuf, dbuf.at[j - 1], cs, cr.at[j - 1], beside(j))

    def opened(buf, slot):
        tail = buf[slot, feats : feats + TAIL, :].astype(F32)
        return buf[slot, 0:feats, :].astype(F32), tail[0:1, :], tail[1:2, :]

    def join_row():
        for j in range(share - 1):
            whole(dbuf.at[j], cr.at[j]).wait()
        parts = [opened(dbuf, j) for j in range(share - 1)]
        mine_norm = cbuf[feats : feats + TAIL, :].astype(F32)
        parts.append((cbuf[0:feats, :].astype(F32), mine_norm[0:1, :], mine_norm[1:2, :]))
        lead_id = parts[0][2]
        for part in parts[1:]:
            lead_id = jnp.minimum(lead_id, part[2])
        sums = [jnp.where(p[2] == lead_id, p[0], 0.0) for p in parts]
        norms = [jnp.where(p[2] == lead_id, p[1], 0.0) for p in parts]
        total, end = payload(sum(sums), sum(norms), lead_id)
        tbuf[0:feats, :] = total
        tbuf[feats : feats + TAIL, :] = end
        for k in range(2):
            send(tbuf, ebuf.at[k], es, er.at[k], along(planes - 1 - k))
        back, back_norm = jnp.zeros((feats, width), F32), jnp.zeros((1, feats), F32)
        for j in range(share - 1):
            source = lax.rem(col_x + share - 1 - j, share)
            keep = (parts[j][2] == last_id) & (source > col_x)
            back += jnp.where(keep, parts[j][0], 0.0)
            back_norm += jnp.where(keep, parts[j][1], 0.0)
        back_s[...] = back
        backn_s[...] = jnp.broadcast_to(back_norm, backn_s.shape)

    per = gq.shape[1]

    def head_of(turn):
        off = ((planes - turn) // 2) * (2 * (turn % 2) - 1)
        return lax.rem(row + off + planes, planes)

    def scatter(turn):
        h = head_of(turn)
        pltpu.make_async_copy(gq.at[h * share + col_x], xin.at[h, col_x], r1.at[h]).start()
        for j in range(1, share):
            to = h * share + lax.rem(col_x + j, share)
            send(gq.at[to], xin.at[h, col_x], s1, r1.at[h], beside(j))

    def row_sum(turn):
        h = head_of(turn)
        whole(xin.at[h], r1.at[h]).wait()
        return h, jnp.sum(xin[h].astype(F32), axis=0).astype(BF16)

    def climb(turn):
        h, part = row_sum(turn)
        zsend[h] = part
        send(zsend.at[h], zin.at[row], s2, r2, {"context": h * share + col_x})

    def backward(turn, _):
        h = head_of(turn)

        outs = []
        for i in range(0, length, step):
            end = i + step
            dn = dn_s[h, i:end, :]
            dd = dd_s[h, i:end, :]
            d_score = dot_nt(dn, vx[WIN : WIN + end, :]) + dd
            d_score = (d_score * mask[i:end, 0:end]).astype(BF16)
            d_phi = dot_nn(d_score, phik[0:end, :])
            d_phi += take[i:end, :] * (dot_nt(dn, state) + dd * norm)
            dphik[0:end, :] += dot_tn(d_score, phi_s[h, i:end, :])
            outs.append((d_phi * slope_s[h, i:end, :]).astype(BF16))
        grad = dot_tn(qb[h], jnp.concatenate(outs, axis=0)).astype(BF16)
        for j in range(share):
            gq[h * share + j] = grad[j * per : (j + 1) * per, :]
        return 0

    def backward_two(t, _):
        backward(2 * t, 0)
        return backward(2 * t + 1, 0)

    lax.fori_loop(0, SPLIT // 2, backward_two, 0)
    join_row()
    for turn in range(SPLIT):
        scatter(turn)
    backward_two(SPLIT // 2, 0)
    scatter(SPLIT)
    scatter(SPLIT + 1)
    backward_two(SPLIT // 2 + 1, 0)
    scatter(SPLIT + 2)
    scatter(SPLIT + 3)
    for turn in range(SPLIT - 1):
        climb(turn)

    back, back_norm = back_s[...], backn_s[0:1, :]
    for k in range(2):
        whole(ebuf.at[k], er.at[k]).wait()
        part = opened(ebuf, k)
        keep = (part[2] == last_id) & (row + k + 1 < planes)
        back += jnp.where(keep, part[0], 0.0)
        back_norm += jnp.where(keep, part[1], 0.0)
    own = jnp.where(columns_of(seg_ref[...]) == last_id, 1.0, 0.0)
    d_phi = dphik[...] + own * (dot_nt(vx[WIN : WIN + length, 0:width], back.astype(BF16)) + back_norm)
    d_pre = (d_phi * slopek[...]).astype(BF16)
    grad = dot_tn(kx[WIN : WIN + length, :], d_pre)
    kpart[...] = grad.reshape(kpart.shape).astype(BF16)

    def piece(ref, peer):
        return ref.at[lax.rem(peer["context"], share)]

    pltpu.make_async_copy(kpart.at[col_x], kxin.at[col_x], r4).start()
    for j in range(1, share):
        send(piece(kpart, beside(j)), kxin.at[col_x], s4, r4, beside(j))
    keys_out[...] = dot_nt(d_pre, fk[...]).astype(BF16)

    for turn in range(SPLIT - 1, heads - 1):
        climb(turn)
    zin[row] = row_sum(heads - 1)[1]
    whole(kxin, r4).wait()
    kmid[...] = jnp.sum(kxin[...].astype(F32), axis=0).astype(BF16)
    pltpu.make_async_copy(kmid, kzin.at[row], r5).start()
    for j in range(1, planes):
        send(kmid, kzin.at[row], s5, r5, along(j))
    whole(zin.at[pl.ds(0, planes - 1)], r2).wait()
    red[...] = jnp.sum(zin[...].astype(F32), axis=0).astype(BF16)
    pltpu.make_async_copy(red, spread.at[here], r3).start()
    for j in range(1, planes):
        send(red, spread.at[here], s3, ra.at[row], along(j))
    for j in range(1, share):
        send(red, spread.at[here], s7, r7, beside(j))

    def pass_on(off):
        source = lax.rem(row + off, planes)
        chunk = spread.at[source * share + col_x]
        whole(chunk, ra.at[source]).wait()
        for j in range(1, share):
            send(chunk, chunk, s7, r7, beside(j))

    order = sorted(range(1, planes), key=lambda o: min(o, planes - o))
    for off in order[:-3]:
        pass_on(off)
    whole(kzin, r5).wait()
    kred[...] = jnp.sum(kzin[...].astype(F32), axis=0).astype(BF16)
    pltpu.make_async_copy(kred, kspread.at[col_x], r6).start()
    for j in range(1, share):
        send(kred, kspread.at[col_x], s6, r6, beside(j))
    for off in order[-3:]:
        pass_on(off)

    for copy in sends:
        copy.wait_send()
    whole(qb.at[:, pl.ds(0, length - rows), :], qs).wait()
    whole(dbuf, cs).wait()
    whole(ebuf, es).wait()
    whole(xin.at[:, pl.ds(0, share - 1)], s1).wait()
    whole(zin.at[pl.ds(0, planes - 1)], s2).wait()
    whole(spread.at[pl.ds(0, planes - 1)], s3).wait()
    whole(kxin.at[pl.ds(0, share - 1)], s4).wait()
    whole(kzin.at[pl.ds(0, planes - 1)], s5).wait()
    whole(kspread.at[pl.ds(0, share - 1)], s6).wait()
    beyond = spread.at[pl.ds(0, (share - 1) * planes)]
    whole(beyond, s7).wait()
    whole(spread.at[here], r3).wait()
    whole(kspread, r6).wait()
    whole(beyond, r7).wait()


def store_kernel(scale, err_in, keys_in, gq_in, gk_in, err_out, keys_out, gq_out, gk_out):
    err_out[...] = err_in[...]
    keys_out[...] = keys_in[...]
    gq_out[...] = gq_in[...].astype(F32) * scale
    gk_out[...] = gk_in[...].astype(F32) * scale


def on_device(queries, keys, values, segments, feat_q, feat_k):
    rows = keys.shape[0]
    split = lax.axis_size("ulysses")
    count = lax.axis_size("context")
    heads, width, feats = feat_q.shape
    length = rows * split
    seg = segments.reshape(1, length)
    key_map = feat_k.reshape(width, feats)
    per = heads * width // count
    share = count // heads
    planes = count // share
    shape = jax.ShapeDtypeStruct
    hbm = pl.BlockSpec(memory_space=pltpu.HBM)
    vmem = pl.BlockSpec(memory_space=pltpu.VMEM)
    dma = pltpu.SemaphoreType.DMA
    stay = functools.partial(pltpu.with_memory_space_constraint, memory_space=pltpu.HBM)
    ext = length + WIN
    packed = feats + TAIL

    outs = pl.pallas_call(
        step_kernel,
        name="step",
        out_shape=(
            shape((length, heads * width), BF16),
            shape((length, width), BF16),
            shape((count, per, feats), BF16),
            shape((share, width // share, feats), BF16),
        ),
        in_specs=[hbm] * 6,
        out_specs=[vmem] * 4,
        scratch_shapes=[
            pltpu.VMEM((1, length), jnp.int32),
            pltpu.VMEM((rows, queries.shape[1]), BF16),
            pltpu.VMEM((heads, length, width), BF16),
            pltpu.VMEM((ext, width), BF16),
            pltpu.VMEM((ext, width), BF16),
            pltpu.VMEM((heads, width, feats), BF16),
            pltpu.VMEM((width, feats), BF16),
            pltpu.VMEM((1, WIN), jnp.int32),
            pltpu.VMEM((packed, width), BF16),
            pltpu.VMEM((REACH, packed, width), BF16),
            pltpu.VMEM((packed, width), BF16),
            pltpu.VMEM((share - 1, packed, width), BF16),
            pltpu.VMEM((packed, width), BF16),
            pltpu.VMEM((2, packed, width), BF16),
            pltpu.VMEM((feats, width), F32),
            pltpu.VMEM((8, feats), F32),
            pltpu.VMEM((length, length), F32),
            pltpu.VMEM((length, 2 * WIN), F32),
            pltpu.VMEM((length, feats), F32),
            pltpu.VMEM((length, feats), BF16),
            pltpu.VMEM((heads, length, feats), BF16),
            pltpu.VMEM((heads, length, feats), BF16),
            pltpu.VMEM((heads, length, feats), F32),
            pltpu.VMEM((heads, length, width), F32),
            pltpu.VMEM((heads, length, 1), F32),
            pltpu.VMEM((heads, length, width), F32),
            pltpu.VMEM((heads, length, width), BF16),
            pltpu.VMEM((heads, length, 1), F32),
            pltpu.VMEM((length, feats), BF16),
            pltpu.VMEM((length, feats), F32),
            pltpu.VMEM((length, feats), F32),
            pltpu.VMEM((feats, width), F32),
            pltpu.VMEM((8, feats), F32),
            pltpu.VMEM((count, per, feats), BF16),
            pltpu.VMEM((planes, share, per, feats), BF16),
            pltpu.VMEM((planes, per, feats), BF16),
            pltpu.VMEM((planes, per, feats), BF16),
            pltpu.VMEM((per, feats), BF16),
            pltpu.VMEM((share, per, feats), BF16),
            pltpu.VMEM((share, per, feats), BF16),
            pltpu.VMEM((per, feats), BF16),
            pltpu.VMEM((planes, per, feats), BF16),
            pltpu.VMEM((per, feats), BF16),
            dma,
            dma((3,)),
            dma((split - 1,)),
            dma((split - 1,)),
            dma,
            dma((split,)),
            dma((split,)),
            dma((heads,)),
            dma((3,)),
            dma((3,)),
            dma((REACH,)),
            dma((REACH,)),
            dma,
            dma((share - 1,)),
            dma,
            dma((2,)),
        ]
        + [dma, dma((heads,))]
        + [dma] * 12
        + [dma((planes,))],
        compiler_params=pltpu.CompilerParams(
            collective_id=0, has_side_effects=True, vmem_limit_bytes=50 * 1024 * 1024
        ),
    )(stay(queries), stay(keys), stay(values), stay(seg), stay(feat_q), stay(key_map))

    errors, grad_keys, grad_q, grad_k = pl.pallas_call(
        functools.partial(store_kernel, 1.0 / math.sqrt(length * count)),
        name="store",
        out_shape=(
            shape((length, heads * width), BF16),
            shape((length, width), BF16),
            shape((count, per, feats), F32),
            shape((share, width // share, feats), F32),
        ),
        in_specs=[vmem] * 4,
        out_specs=[vmem] * 4,
        compiler_params=pltpu.CompilerParams(vmem_limit_bytes=8 * 1024 * 1024),
    )(*outs)
    return (
        errors,
        grad_keys,
        grad_q.reshape(heads, width, feats),
        grad_k.reshape(feat_k.shape),
    )


def solution(mesh):
    in_specs = (
        P(("dp", "context", "ulysses"), None),
        P(("dp", "context", "ulysses"), None),
        P(("dp", "context", "ulysses"), None),
        P(("dp", "context")),
        P("ulysses", None, None),
        P("ulysses", None, None),
    )
    out_specs = (
        P(("dp", "context"), "ulysses"),
        P(("dp", "context"), "ulysses"),
        P(("dp", "ulysses"), None, None),
        P(("dp", "ulysses"), None, None),
    )
    return jax.shard_map(
        on_device, mesh=mesh, in_specs=in_specs, out_specs=out_specs, check_vma=False
    )
```

```python
import functools
import math

import jax
import jax.numpy as jnp
from jax import lax
from jax.experimental import pallas as pl
from jax.experimental.pallas import tpu as pltpu
from jax.sharding import PartitionSpec as P

WIN = 128
JOIN = 3
SPLIT = 4
TAIL = 16
MESH = pl.DeviceIdType.MESH
F32 = jnp.float32
BF16 = jnp.bfloat16


def dot_nn(a, b):
    return lax.dot_general(a, b, (((1,), (0,)), ((), ())), preferred_element_type=F32)


def dot_nt(a, b):
    return lax.dot_general(a, b, (((1,), (1,)), ((), ())), preferred_element_type=F32)


def dot_tn(a, b):
    return lax.dot_general(a, b, (((0,), (0,)), ((), ())), preferred_element_type=F32)


def remote(src, dst, send, recv, **where):
    return pltpu.make_async_remote_copy(
        src_ref=src, dst_ref=dst, send_sem=send, recv_sem=recv, device_id=where, device_id_type=MESH
    )


def whole(ref, sem):
    return pltpu.make_async_copy(ref, ref, sem)


def columns_of(seg_row):
    length = seg_row.shape[1]
    parts = [
        jnp.transpose(jnp.broadcast_to(seg_row[:, i : i + 128].astype(F32), (128, 128)))
        for i in range(0, length, 128)
    ]
    return jnp.concatenate(parts, axis=0)


def payload(state, norm, ident):
    row = lax.broadcasted_iota(jnp.int32, (TAIL, norm.shape[1]), 0)
    tail = jnp.where(row == 0, norm, jnp.where(row == 1, ident, 0.0))
    return state.astype(BF16), tail.astype(BF16)


def step_kernel(
    q_ref, k_ref, v_ref, seg_in, fq_ref, fk_ref,
    err_ref, keys_out, spread, kspread,
    seg_ref, qv, qb, kx, vx, fq, fk, rim_in, sbuf, rbuf, cbuf, dbuf, tbuf, ebuf, ubuf, wbuf, back_s, backn_s,
    mask, bias, take, takeb, lead_s, phi_s, slope_s, num_s, den_s, tea_s, dn_s, dd_s, phik, slopek, dphik, cot, acc,
    gq, xin, zsend, zin, red, kpart, kxin, kmid, kzin, kred,
    ql, fl, ks, vs, qs, kr, vr, qr, rs, rr, xs, xr, cs, cr, es, er, us, ur,
    s1, r1, s2, r2, s3, r3, s4, r4, s5, r5, s6, r6, s7, r7, ra,
):
    here, mine = lax.axis_index("context"), lax.axis_index("ulysses")
    count, split = lax.axis_size("context"), lax.axis_size("ulysses")
    rows = k_ref.shape[0]
    heads, width, feats = fq_ref.shape
    length = rows * split
    wide = heads * width
    step = 256
    inv_scale = 1.0 / math.sqrt(width)

    share = count // heads
    row, col_x = here // share, lax.rem(here, share)
    planes = count // share

    def beside(j):
        return {"context": row * share + lax.rem(col_x + j, share)}

    def along(j):
        return {"context": lax.rem(row + j, planes) * share + col_x}

    barrier = pltpu.get_barrier_semaphore()
    near = [{"ulysses": lax.rem(mine + j, split)} for j in range(1, split)]
    near += [beside(j) for j in range(1, share)]
    near += [along(j) for j in range(1, planes)]
    near += [{"context": lax.rem(here + k, count)} for k in (1, count - 1)]
    for peer in near:
        pl.semaphore_signal(barrier, inc=1, device_id=peer, device_id_type=MESH)

    def place(start):
        return pl.ds(pl.multiple_of(start + mine * rows, 128), rows)

    def lanes(who, size):
        return pl.ds(pl.multiple_of(who * size, 128), size)

    load_seg = pltpu.make_async_copy(seg_in, seg_ref, fl.at[2])
    load_seg.start()
    front = pl.ds(0, width)
    small = ((k_ref, kx, ks, kr), (v_ref, vx, vs, vr))
    for src, dst, _, recv in small:
        pltpu.make_async_copy(
            src.at[:, lanes(mine, width)], dst.at[place(WIN), front], recv.at[mine]
        ).start()
    load_q = pltpu.make_async_copy(q_ref, qv, ql)
    load_q.start()
    loads = [pltpu.make_async_copy(fq_ref, fq, fl.at[0]), pltpu.make_async_copy(fk_ref, fk, fl.at[1])]
    for copy in loads:
        copy.start()

    pl.semaphore_wait(barrier, len(near))

    sends = []
    for src, dst, send, recv in small:
        for j in range(1, split):
            peer = lax.rem(mine + j, split)
            copy = remote(
                src.at[:, lanes(peer, width)], dst.at[place(WIN), front], send.at[j - 1],
                recv.at[mine], ulysses=peer,
            )
            copy.start()
            sends.append(copy)

    load_q.wait()
    for h in range(heads):
        pltpu.make_async_copy(
            qv.at[:, lanes(mine * heads + h, width)], qb.at[h, place(0), :], qr.at[h]
        ).start()

    def send_q(h, _):
        for j in range(1, split):
            peer = lax.rem(mine + j, split)
            remote(
                qv.at[:, lanes(peer * heads + h, width)], qb.at[h, place(0), :], qs, qr.at[h],
                ulysses=peer,
            ).start()
        return 0

    lax.fori_loop(0, heads, send_q, 0)

    load_seg.wait()
    seg_row = seg_ref[...]
    rows_f = seg_row.astype(F32)
    first_id = jnp.min(seg_row, axis=1, keepdims=True).astype(F32)
    last_id = jnp.max(seg_row, axis=1, keepdims=True).astype(F32)
    seg_col = columns_of(seg_row)
    take[...] = jnp.where(seg_col == first_id, 1.0, 0.0)
    takeb[...] = jnp.where(seg_col == first_id, 1.0, 0.0).astype(BF16)
    r = lax.broadcasted_iota(jnp.int32, (128, 128), 0)
    c = lax.broadcasted_iota(jnp.int32, (128, 128), 1)
    for i in range(0, length, 128):
        col = seg_col[i : i + 128, :]
        for j in range(0, length, 128):
            if j > i:
                mask[i : i + 128, j : j + 128] = jnp.zeros((128, 128), F32)
                continue
            same = col == rows_f[:, j : j + 128]
            if j == i:
                same = same & (c <= r)
            mask[i : i + 128, j : j + 128] = jnp.where(same, 1.0, 0.0)
        if i:
            bias[i : i + 128, 0:128] = jnp.where(
                (col == rows_f[:, i - 128 : i]) & (c > r), 0.0, -1e30
            )
        bias[i : i + 128, 128:256] = jnp.where(
            (col == rows_f[:, i : i + 128]) & (c <= r), 0.0, -1e30
        )
    cot[...] = jnp.zeros_like(cot)
    acc[...] = jnp.zeros_like(acc)
    dphik[...] = jnp.zeros_like(dphik)
    for copy in loads:
        copy.wait()
    after = lax.rem(here + 1, count)
    edge, rim = pl.ds(length, WIN), pl.ds(0, WIN)
    rims = [
        remote(seg_ref.at[:, pl.ds(length - WIN, WIN)], rim_in, rs.at[2], rr.at[2], context=after),
        remote(kx.at[edge, front], kx.at[rim, front], rs.at[0], rr.at[0], context=after),
        remote(vx.at[edge, front], vx.at[rim, front], rs.at[1], rr.at[1], context=after),
    ]
    rims[0].start()

    def arrived(ref, sems, who):
        whole(ref.at[pl.ds(WIN + who * rows, rows), front], sems.at[who]).wait()

    arrived(kx, kr, split - 1)
    rims[1].start()
    arrived(vx, vr, split - 1)
    rims[2].start()
    for who in range(split - 1):
        arrived(kx, kr, who)
    for who in range(split - 1):
        arrived(vx, vr, who)

    pre = dot_nn(kx[WIN : WIN + length, :], fk[...])
    low = jnp.exp(jnp.minimum(pre, 0.0))
    phi = jnp.where(pre > 0, pre + 1.0, low).astype(BF16)
    phik[...] = phi
    slopek[...] = jnp.where(pre > 0, 1.0, low)
    tail = jnp.where(seg_col == last_id, phi.astype(F32), 0.0)
    state, end = payload(
        dot_tn(tail.astype(BF16), vx[WIN : WIN + length, 0:width]),
        jnp.sum(tail, axis=0, keepdims=True),
        last_id,
    )
    sbuf[0:feats, :] = state
    sbuf[feats : feats + TAIL, :] = end
    def send(src, dst, send_sem, recv_sem, peer):
        pltpu.make_async_remote_copy(
            src_ref=src, dst_ref=dst, send_sem=send_sem, recv_sem=recv_sem,
            device_id=peer, device_id_type=MESH,
        ).start()

    def opened(ref):
        tail = ref[feats : feats + TAIL, :].astype(F32)
        return ref[0:feats, :].astype(F32), tail[0:1, :], tail[1:2, :]

    def join_row(own, buf, sems, out, far, out_sem, far_sems, ident, ahead):
        for j in range(share - 1):
            whole(buf.at[j], sems.at[j]).wait()
        parts = [opened(buf.at[j]) for j in range(share - 1)]
        every = parts + [opened(own)]
        lead_id = every[0][2]
        for part in every[1:]:
            lead_id = jnp.maximum(lead_id, part[2]) if ahead else jnp.minimum(lead_id, part[2])
        sums = [jnp.where(p[2] == lead_id, p[0], 0.0) for p in every]
        norms = [jnp.where(p[2] == lead_id, p[1], 0.0) for p in every]
        total, end = payload(sum(sums), sum(norms), lead_id)
        out[0:feats, :] = total
        out[feats : feats + TAIL, :] = end
        for k in range(2):
            send(out, far.at[k], out_sem, far_sems.at[k], along(k + 1 if ahead else planes - 1 - k))
        got, got_norm = jnp.zeros((feats, width), F32), jnp.zeros((1, feats), F32)
        for j in range(share - 1):
            source = lax.rem(col_x + share - 1 - j, share)
            side = source < col_x if ahead else source > col_x
            keep = (parts[j][2] == ident) & side
            got += jnp.where(keep, parts[j][0], 0.0)
            got_norm += jnp.where(keep, parts[j][1], 0.0)
        back_s[...] = got
        backn_s[...] = jnp.broadcast_to(got_norm, backn_s.shape)

    def from_rows(far, far_sems, ident, ahead):
        got, got_norm = back_s[...], backn_s[0:1, :]
        for k in range(2):
            whole(far.at[k], far_sems.at[k]).wait()
            part = opened(far.at[k])
            inside = row > k if ahead else row + k + 1 < planes
            keep = (part[2] == ident) & inside
            got += jnp.where(keep, part[0], 0.0)
            got_norm += jnp.where(keep, part[1], 0.0)
        return got, got_norm

    for j in range(1, share):
        send(sbuf, rbuf.at[j - 1], xs, xr.at[j - 1], beside(j))

    def linear(h):
        q = qb[h]
        pre = dot_nn(q, fq[h])
        low = jnp.exp(jnp.minimum(pre, 0.0))
        phi = jnp.where(pre > 0, pre + 1.0, low).astype(BF16)
        slope_s[h] = jnp.where(pre > 0, 1.0, low)
        phi_s[h] = phi
        lead_s[h] = phi * takeb[...]
        for i in range(0, length, step):
            end = i + step
            score = dot_nt(phi[i:end], phik[0:end, :]) * mask[i:end, 0:end]
            num_s[h, i:end, :] = dot_nn(score.astype(BF16), vx[WIN : WIN + end, :])
            den_s[h, i:end, :] = jnp.sum(score, axis=1, keepdims=True)

    def window(h):
        q = qb[h]
        for j in range(0, length, 128):
            logits = dot_nt(q[j : j + 128], kx[j : j + 256, :]) * inv_scale
            logits += bias[j : j + 128, :]
            probs = jnp.exp(logits - jnp.max(logits, axis=1, keepdims=True))
            total = jnp.sum(probs, axis=1, keepdims=True)
            tea_s[h, j : j + 128, :] = dot_nn(probs.astype(BF16), vx[j : j + 256, :]) * (1.0 / total)

    def forward(h, _):
        whole(qb.at[h], qr.at[h]).wait()
        linear(h)
        window(h)
        return 0

    for h in range(2):
        whole(qb.at[h], qr.at[h]).wait()
        linear(h)
    for copy in rims:
        copy.wait()
    rim_f = jnp.where(here > 0, rim_in[...], -1).astype(F32)
    bias[0:128, 0:128] = jnp.where((seg_col[0:128, :] == rim_f) & (c > r), 0.0, -1e30)

    for h in range(2):
        window(h)
    lax.fori_loop(2, JOIN, forward, 0)
    join_row(sbuf, rbuf, xr, ubuf, wbuf, us, ur, first_id, True)
    lax.fori_loop(JOIN, heads, forward, 0)
    state, norm = from_rows(wbuf, ur, first_id, True)
    state = state.astype(BF16)

    def meet(h, _):
        lead = lead_s[h]
        lead_f = lead.astype(F32)
        inv = 1.0 / (den_s[h] + jnp.sum(lead_f * norm, axis=1, keepdims=True))
        student = (num_s[h] + dot_nn(lead, state)) * inv
        gap = student - tea_s[h]
        err_ref[:, lanes(h, width)] = gap.astype(BF16)
        up = 32.0 * gap
        dn = (up * inv).astype(BF16)
        dd = -jnp.sum(up * student, axis=1, keepdims=True) * inv
        dn_s[h] = dn
        dd_s[h] = dd
        acc[...] += jnp.sum((lead_f * dd).reshape(length // 8, 8, feats), axis=0)
        cot[...] += dot_tn(lead, dn)
        return 0

    def meet_two(t, _):
        meet(2 * t, 0)
        return meet(2 * t + 1, 0)

    lax.fori_loop(0, heads // 2, meet_two, 0)
    total, end = payload(cot[...], jnp.sum(acc[...], axis=0, keepdims=True), first_id)
    cbuf[0:feats, :] = total
    cbuf[feats : feats + TAIL, :] = end

    for j in range(1, share):
        send(cbuf, dbuf.at[j - 1], cs, cr.at[j - 1], beside(j))

    per = gq.shape[1]

    def head_of(turn):
        off = ((planes - turn) // 2) * (2 * (turn % 2) - 1)
        return lax.rem(row + off + planes, planes)

    def scatter(turn):
        h = head_of(turn)
        pltpu.make_async_copy(gq.at[h * share + col_x], xin.at[h, col_x], r1.at[h]).start()
        for j in range(1, share):
            to = h * share + lax.rem(col_x + j, share)
            send(gq.at[to], xin.at[h, col_x], s1, r1.at[h], beside(j))

    def row_sum(turn):
        h = head_of(turn)
        whole(xin.at[h], r1.at[h]).wait()
        return h, jnp.sum(xin[h].astype(F32), axis=0).astype(BF16)

    def climb(turn):
        h, part = row_sum(turn)
        zsend[h] = part
        send(zsend.at[h], zin.at[row], s2, r2, {"context": h * share + col_x})

    def backward(turn, _):
        h = head_of(turn)

        outs = []
        for i in range(0, length, step):
            end = i + step
            dn = dn_s[h, i:end, :]
            dd = dd_s[h, i:end, :]
            d_score = dot_nt(dn, vx[WIN : WIN + end, :]) + dd
            d_score = (d_score * mask[i:end, 0:end]).astype(BF16)
            d_phi = dot_nn(d_score, phik[0:end, :])
            d_phi += take[i:end, :] * (dot_nt(dn, state) + dd * norm)
            dphik[0:end, :] += dot_tn(d_score, phi_s[h, i:end, :])
            outs.append((d_phi * slope_s[h, i:end, :]).astype(BF16))
        grad = dot_tn(qb[h], jnp.concatenate(outs, axis=0)).astype(BF16)
        for j in range(share):
            gq[h * share + j] = grad[j * per : (j + 1) * per, :]
        return 0

    def backward_two(t, _):
        backward(2 * t, 0)
        return backward(2 * t + 1, 0)

    lax.fori_loop(0, SPLIT // 2, backward_two, 0)
    for turn in range(SPLIT):
        scatter(turn)
    backward_two(SPLIT // 2, 0)
    join_row(cbuf, dbuf, cr, tbuf, ebuf, es, er, last_id, False)
    scatter(SPLIT)
    scatter(SPLIT + 1)
    backward_two(SPLIT // 2 + 1, 0)
    scatter(SPLIT + 2)
    scatter(SPLIT + 3)
    for turn in range(SPLIT - 1):
        climb(turn)

    back, back_norm = from_rows(ebuf, er, last_id, False)
    own = jnp.where(columns_of(seg_ref[...]) == last_id, 1.0, 0.0)
    d_phi = dphik[...] + own * (dot_nt(vx[WIN : WIN + length, 0:width], back.astype(BF16)) + back_norm)
    d_pre = (d_phi * slopek[...]).astype(BF16)
    grad = dot_tn(kx[WIN : WIN + length, :], d_pre)
    kpart[...] = grad.reshape(kpart.shape).astype(BF16)

    def piece(ref, peer):
        return ref.at[lax.rem(peer["context"], share)]

    pltpu.make_async_copy(kpart.at[col_x], kxin.at[col_x], r4).start()
    for j in range(1, share):
        send(piece(kpart, beside(j)), kxin.at[col_x], s4, r4, beside(j))
    keys_out[...] = dot_nt(d_pre, fk[...]).astype(BF16)

    for turn in range(SPLIT - 1, heads - 1):
        climb(turn)
    zin[row] = row_sum(heads - 1)[1]
    whole(kxin, r4).wait()
    kmid[...] = jnp.sum(kxin[...].astype(F32), axis=0).astype(BF16)
    pltpu.make_async_copy(kmid, kzin.at[row], r5).start()
    for j in range(1, planes):
        send(kmid, kzin.at[row], s5, r5, along(j))
    whole(zin.at[pl.ds(0, planes - 1)], r2).wait()
    red[...] = jnp.sum(zin[...].astype(F32), axis=0).astype(BF16)
    pltpu.make_async_copy(red, spread.at[here], r3).start()
    for j in range(1, planes):
        send(red, spread.at[here], s3, ra.at[row], along(j))
    for j in range(1, share):
        send(red, spread.at[here], s7, r7, beside(j))

    def pass_on(off):
        source = lax.rem(row + off, planes)
        chunk = spread.at[source * share + col_x]
        whole(chunk, ra.at[source]).wait()
        for j in range(1, share):
            send(chunk, chunk, s7, r7, beside(j))

    order = sorted(range(1, planes), key=lambda o: min(o, planes - o))
    for off in order[:-3]:
        pass_on(off)
    whole(kzin, r5).wait()
    kred[...] = jnp.sum(kzin[...].astype(F32), axis=0).astype(BF16)
    pltpu.make_async_copy(kred, kspread.at[col_x], r6).start()
    for j in range(1, share):
        send(kred, kspread.at[col_x], s6, r6, beside(j))
    for off in order[-3:]:
        pass_on(off)

    for copy in sends:
        copy.wait_send()
    whole(qb.at[:, pl.ds(0, length - rows), :], qs).wait()
    whole(rbuf, xs).wait()
    whole(wbuf, us).wait()
    whole(dbuf, cs).wait()
    whole(ebuf, es).wait()
    whole(xin.at[:, pl.ds(0, share - 1)], s1).wait()
    whole(zin.at[pl.ds(0, planes - 1)], s2).wait()
    whole(spread.at[pl.ds(0, planes - 1)], s3).wait()
    whole(kxin.at[pl.ds(0, share - 1)], s4).wait()
    whole(kzin.at[pl.ds(0, planes - 1)], s5).wait()
    whole(kspread.at[pl.ds(0, share - 1)], s6).wait()
    beyond = spread.at[pl.ds(0, (share - 1) * planes)]
    whole(beyond, s7).wait()
    whole(spread.at[here], r3).wait()
    whole(kspread, r6).wait()
    whole(beyond, r7).wait()


def store_kernel(scale, err_in, keys_in, gq_in, gk_in, err_out, keys_out, gq_out, gk_out):
    err_out[...] = err_in[...]
    keys_out[...] = keys_in[...]
    gq_out[...] = gq_in[...].astype(F32) * scale
    gk_out[...] = gk_in[...].astype(F32) * scale


def on_device(queries, keys, values, segments, feat_q, feat_k):
    rows = keys.shape[0]
    split = lax.axis_size("ulysses")
    count = lax.axis_size("context")
    heads, width, feats = feat_q.shape
    length = rows * split
    seg = segments.reshape(1, length)
    key_map = feat_k.reshape(width, feats)
    per = heads * width // count
    share = count // heads
    planes = count // share
    shape = jax.ShapeDtypeStruct
    hbm = pl.BlockSpec(memory_space=pltpu.HBM)
    vmem = pl.BlockSpec(memory_space=pltpu.VMEM)
    dma = pltpu.SemaphoreType.DMA
    stay = functools.partial(pltpu.with_memory_space_constraint, memory_space=pltpu.HBM)
    ext = length + WIN
    packed = feats + TAIL

    outs = pl.pallas_call(
        step_kernel,
        name="step",
        out_shape=(
            shape((length, heads * width), BF16),
            shape((length, width), BF16),
            shape((count, per, feats), BF16),
            shape((share, width // share, feats), BF16),
        ),
        in_specs=[hbm] * 6,
        out_specs=[vmem] * 4,
        scratch_shapes=[
            pltpu.VMEM((1, length), jnp.int32),
            pltpu.VMEM((rows, queries.shape[1]), BF16),
            pltpu.VMEM((heads, length, width), BF16),
            pltpu.VMEM((ext, width), BF16),
            pltpu.VMEM((ext, width), BF16),
            pltpu.VMEM((heads, width, feats), BF16),
            pltpu.VMEM((width, feats), BF16),
            pltpu.VMEM((1, WIN), jnp.int32),
            pltpu.VMEM((packed, width), BF16),
            pltpu.VMEM((share - 1, packed, width), BF16),
            pltpu.VMEM((packed, width), BF16),
            pltpu.VMEM((share - 1, packed, width), BF16),
            pltpu.VMEM((packed, width), BF16),
            pltpu.VMEM((2, packed, width), BF16),
            pltpu.VMEM((packed, width), BF16),
            pltpu.VMEM((2, packed, width), BF16),
            pltpu.VMEM((feats, width), F32),
            pltpu.VMEM((8, feats), F32),
            pltpu.VMEM((length, length), F32),
            pltpu.VMEM((length, 2 * WIN), F32),
            pltpu.VMEM((length, feats), F32),
            pltpu.VMEM((length, feats), BF16),
            pltpu.VMEM((heads, length, feats), BF16),
            pltpu.VMEM((heads, length, feats), BF16),
            pltpu.VMEM((heads, length, feats), F32),
            pltpu.VMEM((heads, length, width), F32),
            pltpu.VMEM((heads, length, 1), F32),
            pltpu.VMEM((heads, length, width), F32),
            pltpu.VMEM((heads, length, width), BF16),
            pltpu.VMEM((heads, length, 1), F32),
            pltpu.VMEM((length, feats), BF16),
            pltpu.VMEM((length, feats), F32),
            pltpu.VMEM((length, feats), F32),
            pltpu.VMEM((feats, width), F32),
            pltpu.VMEM((8, feats), F32),
            pltpu.VMEM((count, per, feats), BF16),
            pltpu.VMEM((planes, share, per, feats), BF16),
            pltpu.VMEM((planes, per, feats), BF16),
            pltpu.VMEM((planes, per, feats), BF16),
            pltpu.VMEM((per, feats), BF16),
            pltpu.VMEM((share, per, feats), BF16),
            pltpu.VMEM((share, per, feats), BF16),
            pltpu.VMEM((per, feats), BF16),
            pltpu.VMEM((planes, per, feats), BF16),
            pltpu.VMEM((per, feats), BF16),
            dma,
            dma((3,)),
            dma((split - 1,)),
            dma((split - 1,)),
            dma,
            dma((split,)),
            dma((split,)),
            dma((heads,)),
            dma((3,)),
            dma((3,)),
            dma,
            dma((share - 1,)),
            dma,
            dma((share - 1,)),
            dma,
            dma((2,)),
            dma,
            dma((2,)),
        ]
        + [dma, dma((heads,))]
        + [dma] * 12
        + [dma((planes,))],
        compiler_params=pltpu.CompilerParams(
            collective_id=0, has_side_effects=True, vmem_limit_bytes=50 * 1024 * 1024
        ),
    )(stay(queries), stay(keys), stay(values), stay(seg), stay(feat_q), stay(key_map))

    errors, grad_keys, grad_q, grad_k = pl.pallas_call(
        functools.partial(store_kernel, 1.0 / math.sqrt(length * count)),
        name="store",
        out_shape=(
            shape((length, heads * width), BF16),
            shape((length, width), BF16),
            shape((count, per, feats), F32),
            shape((share, width // share, feats), F32),
        ),
        in_specs=[vmem] * 4,
        out_specs=[vmem] * 4,
        compiler_params=pltpu.CompilerParams(vmem_limit_bytes=8 * 1024 * 1024),
    )(*outs)
    return (
        errors,
        grad_keys,
        grad_q.reshape(heads, width, feats),
        grad_k.reshape(feat_k.shape),
    )


def solution(mesh):
    in_specs = (
        P(("dp", "context", "ulysses"), None),
        P(("dp", "context", "ulysses"), None),
        P(("dp", "context", "ulysses"), None),
        P(("dp", "context")),
        P("ulysses", None, None),
        P("ulysses", None, None),
    )
    out_specs = (
        P(("dp", "context"), "ulysses"),
        P(("dp", "context"), "ulysses"),
        P(("dp", "ulysses"), None, None),
        P(("dp", "ulysses"), None, None),
    )
    return jax.shard_map(
        on_device, mesh=mesh, in_specs=in_specs, out_specs=out_specs, check_vma=False
    )
```

```python
import functools
import math

import jax
import jax.numpy as jnp
from jax import lax
from jax.experimental import pallas as pl
from jax.experimental.pallas import tpu as pltpu
from jax.sharding import PartitionSpec as P

WIN = 128
JOIN = 3
SPLIT = 4
TAIL = 16
MESH = pl.DeviceIdType.MESH
F32 = jnp.float32
BF16 = jnp.bfloat16


def dot_nn(a, b):
    return lax.dot_general(a, b, (((1,), (0,)), ((), ())), preferred_element_type=F32)


def dot_nt(a, b):
    return lax.dot_general(a, b, (((1,), (1,)), ((), ())), preferred_element_type=F32)


def dot_tn(a, b):
    return lax.dot_general(a, b, (((0,), (0,)), ((), ())), preferred_element_type=F32)


def remote(src, dst, send, recv, **where):
    return pltpu.make_async_remote_copy(
        src_ref=src, dst_ref=dst, send_sem=send, recv_sem=recv, device_id=where, device_id_type=MESH
    )


def whole(ref, sem):
    return pltpu.make_async_copy(ref, ref, sem)


def columns_of(seg_row):
    length = seg_row.shape[1]
    parts = [
        jnp.transpose(jnp.broadcast_to(seg_row[:, i : i + 128].astype(F32), (128, 128)))
        for i in range(0, length, 128)
    ]
    return jnp.concatenate(parts, axis=0)


def payload(state, norm, ident):
    row = lax.broadcasted_iota(jnp.int32, (TAIL, norm.shape[1]), 0)
    tail = jnp.where(row == 0, norm, jnp.where(row == 1, ident, 0.0))
    return state.astype(BF16), tail.astype(BF16)


def step_kernel(
    q_ref, k_ref, v_ref, seg_in, fq_ref, fk_ref,
    err_ref, keys_out, spread, kspread,
    seg_ref, qv, qb, kx, vx, fq, fk, rim_in, sbuf, rbuf, cbuf, dbuf, tbuf, ebuf, ubuf, wbuf, back_s, backn_s,
    mask, bias, take, takeb, lead_s, phi_s, slope_s, num_s, den_s, tea_s, dn_s, dd_s, phik, slopek, dphik, cot, acc,
    gq, xin, zsend, zin, red, kpart, kxin, kmid, kzin, kred,
    ql, fl, ks, vs, qs, kr, vr, qr, rs, rr, xs, xr, cs, cr, es, er, us, ur,
    s1, r1, s2, r2, s3, r3, s4, r4, s5, r5, s6, r6, s7, r7, ra,
):
    here, mine = lax.axis_index("context"), lax.axis_index("ulysses")
    count, split = lax.axis_size("context"), lax.axis_size("ulysses")
    rows = k_ref.shape[0]
    heads, width, feats = fq_ref.shape
    length = rows * split
    wide = heads * width
    step = 256
    inv_scale = 1.0 / math.sqrt(width)

    share = count // heads
    row, col_x = here // share, lax.rem(here, share)
    planes = count // share

    def beside(j):
        return {"context": row * share + lax.rem(col_x + j, share)}

    def along(j):
        return {"context": lax.rem(row + j, planes) * share + col_x}

    barrier = pltpu.get_barrier_semaphore()
    near = [{"ulysses": lax.rem(mine + j, split)} for j in range(1, split)]
    near += [beside(j) for j in range(1, share)]
    near += [along(j) for j in range(1, planes)]
    near += [{"context": lax.rem(here + k, count)} for k in (1, count - 1)]
    for peer in near:
        pl.semaphore_signal(barrier, inc=1, device_id=peer, device_id_type=MESH)

    def place(start):
        return pl.ds(pl.multiple_of(start + mine * rows, 128), rows)

    def lanes(who, size):
        return pl.ds(pl.multiple_of(who * size, 128), size)

    load_seg = pltpu.make_async_copy(seg_in, seg_ref, fl.at[2])
    load_seg.start()
    front = pl.ds(0, width)
    small = ((k_ref, kx, ks, kr), (v_ref, vx, vs, vr))
    for src, dst, _, recv in small:
        pltpu.make_async_copy(
            src.at[:, lanes(mine, width)], dst.at[place(WIN), front], recv.at[mine]
        ).start()
    load_q = pltpu.make_async_copy(q_ref, qv, ql)
    load_q.start()
    loads = [pltpu.make_async_copy(fq_ref, fq, fl.at[0]), pltpu.make_async_copy(fk_ref, fk, fl.at[1])]
    for copy in loads:
        copy.start()

    pl.semaphore_wait(barrier, len(near))

    sends = []
    for src, dst, send, recv in small:
        for j in range(1, split):
            peer = lax.rem(mine + j, split)
            copy = remote(
                src.at[:, lanes(peer, width)], dst.at[place(WIN), front], send.at[j - 1],
                recv.at[mine], ulysses=peer,
            )
            copy.start()
            sends.append(copy)

    load_q.wait()
    for h in range(heads):
        pltpu.make_async_copy(
            qv.at[:, lanes(mine * heads + h, width)], qb.at[h, place(0), :], qr.at[h]
        ).start()

    def send_q(h, _):
        for j in range(1, split):
            peer = lax.rem(mine + j, split)
            remote(
                qv.at[:, lanes(peer * heads + h, width)], qb.at[h, place(0), :], qs, qr.at[h],
                ulysses=peer,
            ).start()
        return 0

    lax.fori_loop(0, heads, send_q, 0)

    load_seg.wait()
    seg_row = seg_ref[...]
    rows_f = seg_row.astype(F32)
    first_id = jnp.min(seg_row, axis=1, keepdims=True).astype(F32)
    last_id = jnp.max(seg_row, axis=1, keepdims=True).astype(F32)
    seg_col = columns_of(seg_row)
    take[...] = jnp.where(seg_col == first_id, 1.0, 0.0)
    takeb[...] = jnp.where(seg_col == first_id, 1.0, 0.0).astype(BF16)
    r = lax.broadcasted_iota(jnp.int32, (128, 128), 0)
    c = lax.broadcasted_iota(jnp.int32, (128, 128), 1)
    for i in range(0, length, 128):
        col = seg_col[i : i + 128, :]
        for j in range(0, length, 128):
            if j > i:
                mask[i : i + 128, j : j + 128] = jnp.zeros((128, 128), F32)
                continue
            same = col == rows_f[:, j : j + 128]
            if j == i:
                same = same & (c <= r)
            mask[i : i + 128, j : j + 128] = jnp.where(same, 1.0, 0.0)
        if i:
            bias[i : i + 128, 0:128] = jnp.where(
                (col == rows_f[:, i - 128 : i]) & (c > r), 0.0, -1e30
            )
        bias[i : i + 128, 128:256] = jnp.where(
            (col == rows_f[:, i : i + 128]) & (c <= r), 0.0, -1e30
        )
    cot[...] = jnp.zeros_like(cot)
    acc[...] = jnp.zeros_like(acc)
    dphik[...] = jnp.zeros_like(dphik)
    for copy in loads:
        copy.wait()
    after = lax.rem(here + 1, count)
    edge, rim = pl.ds(length, WIN), pl.ds(0, WIN)
    rims = [
        remote(seg_ref.at[:, pl.ds(length - WIN, WIN)], rim_in, rs.at[2], rr.at[2], context=after),
        remote(kx.at[edge, front], kx.at[rim, front], rs.at[0], rr.at[0], context=after),
        remote(vx.at[edge, front], vx.at[rim, front], rs.at[1], rr.at[1], context=after),
    ]
    rims[0].start()

    def arrived(ref, sems, who):
        whole(ref.at[pl.ds(WIN + who * rows, rows), front], sems.at[who]).wait()

    arrived(kx, kr, split - 1)
    rims[1].start()
    arrived(vx, vr, split - 1)
    rims[2].start()
    for who in range(split - 1):
        arrived(kx, kr, who)
    for who in range(split - 1):
        arrived(vx, vr, who)

    pre = dot_nn(kx[WIN : WIN + length, :], fk[...])
    low = jnp.exp(jnp.minimum(pre, 0.0))
    phi = jnp.where(pre > 0, pre + 1.0, low).astype(BF16)
    phik[...] = phi
    slopek[...] = jnp.where(pre > 0, 1.0, low)
    tail = jnp.where(seg_col == last_id, phi.astype(F32), 0.0)
    state, end = payload(
        dot_tn(tail.astype(BF16), vx[WIN : WIN + length, 0:width]),
        jnp.sum(tail, axis=0, keepdims=True),
        last_id,
    )
    sbuf[0:feats, :] = state
    sbuf[feats : feats + TAIL, :] = end
    def send(src, dst, send_sem, recv_sem, peer):
        pltpu.make_async_remote_copy(
            src_ref=src, dst_ref=dst, send_sem=send_sem, recv_sem=recv_sem,
            device_id=peer, device_id_type=MESH,
        ).start()

    def opened(ref):
        tail = ref[feats : feats + TAIL, :].astype(F32)
        return ref[0:feats, :].astype(F32), tail[0:1, :], tail[1:2, :]

    def join_row(own, buf, sems, out, far, out_sem, far_sems, ident, ahead):
        for j in range(share - 1):
            whole(buf.at[j], sems.at[j]).wait()
        parts = [opened(buf.at[j]) for j in range(share - 1)]
        every = parts + [opened(own)]
        lead_id = every[0][2]
        for part in every[1:]:
            lead_id = jnp.maximum(lead_id, part[2]) if ahead else jnp.minimum(lead_id, part[2])
        sums = [jnp.where(p[2] == lead_id, p[0], 0.0) for p in every]
        norms = [jnp.where(p[2] == lead_id, p[1], 0.0) for p in every]
        total, end = payload(sum(sums), sum(norms), lead_id)
        out[0:feats, :] = total
        out[feats : feats + TAIL, :] = end
        for k in range(2):
            send(out, far.at[k], out_sem, far_sems.at[k], along(k + 1 if ahead else planes - 1 - k))
        got, got_norm = jnp.zeros((feats, width), F32), jnp.zeros((1, feats), F32)
        for j in range(share - 1):
            source = lax.rem(col_x + share - 1 - j, share)
            side = source < col_x if ahead else source > col_x
            keep = (parts[j][2] == ident) & side
            got += jnp.where(keep, parts[j][0], 0.0)
            got_norm += jnp.where(keep, parts[j][1], 0.0)
        back_s[...] = got
        backn_s[...] = jnp.broadcast_to(got_norm, backn_s.shape)

    def from_rows(far, far_sems, ident, ahead):
        got, got_norm = back_s[...], backn_s[0:1, :]
        for k in range(2):
            whole(far.at[k], far_sems.at[k]).wait()
            part = opened(far.at[k])
            inside = row > k if ahead else row + k + 1 < planes
            keep = (part[2] == ident) & inside
            got += jnp.where(keep, part[0], 0.0)
            got_norm += jnp.where(keep, part[1], 0.0)
        return got, got_norm

    for j in range(1, share):
        send(sbuf, rbuf.at[j - 1], xs, xr.at[j - 1], beside(j))

    def linear(h):
        q = qb[h]
        pre = dot_nn(q, fq[h])
        low = jnp.exp(jnp.minimum(pre, 0.0))
        phi = jnp.where(pre > 0, pre + 1.0, low).astype(BF16)
        slope_s[h] = jnp.where(pre > 0, 1.0, low)
        phi_s[h] = phi
        lead_s[h] = phi * takeb[...]
        for i in range(0, length, step):
            end = i + step
            score = dot_nt(phi[i:end], phik[0:end, :]) * mask[i:end, 0:end]
            num_s[h, i:end, :] = dot_nn(score.astype(BF16), vx[WIN : WIN + end, :])
            den_s[h, i:end, :] = jnp.sum(score, axis=1, keepdims=True)

    def window(h):
        q = qb[h]
        for j in range(0, length, 128):
            logits = dot_nt(q[j : j + 128], kx[j : j + 256, :]) * inv_scale
            logits += bias[j : j + 128, :]
            probs = jnp.exp(logits - jnp.max(logits, axis=1, keepdims=True))
            total = jnp.sum(probs, axis=1, keepdims=True)
            tea_s[h, j : j + 128, :] = dot_nn(probs.astype(BF16), vx[j : j + 256, :]) * (1.0 / total)

    def forward(h, _):
        whole(qb.at[h], qr.at[h]).wait()
        linear(h)
        window(h)
        return 0

    for h in range(2):
        whole(qb.at[h], qr.at[h]).wait()
        linear(h)
    for copy in rims:
        copy.wait()
    rim_f = jnp.where(here > 0, rim_in[...], -1).astype(F32)
    bias[0:128, 0:128] = jnp.where((seg_col[0:128, :] == rim_f) & (c > r), 0.0, -1e30)

    for h in range(2):
        window(h)
    lax.fori_loop(2, JOIN, forward, 0)
    join_row(sbuf, rbuf, xr, ubuf, wbuf, us, ur, first_id, True)
    lax.fori_loop(JOIN, heads - 2, forward, 0)
    state, norm = from_rows(wbuf, ur, first_id, True)
    state = state.astype(BF16)

    def meet(h, _):
        lead = lead_s[h]
        lead_f = lead.astype(F32)
        inv = 1.0 / (den_s[h] + jnp.sum(lead_f * norm, axis=1, keepdims=True))
        student = (num_s[h] + dot_nn(lead, state)) * inv
        gap = student - tea_s[h]
        err_ref[:, lanes(h, width)] = gap.astype(BF16)
        up = 32.0 * gap
        dn = (up * inv).astype(BF16)
        dd = -jnp.sum(up * student, axis=1, keepdims=True) * inv
        dn_s[h] = dn
        dd_s[h] = dd
        acc[...] += jnp.sum((lead_f * dd).reshape(length // 8, 8, feats), axis=0)
        cot[...] += dot_tn(lead, dn)
        return 0

    def meet_two(t, _):
        meet(2 * t, 0)
        return meet(2 * t + 1, 0)

    def forward_meet(t, _):
        h = heads - 2 + t
        meet(2 * t, 0)
        whole(qb.at[h], qr.at[h]).wait()
        meet(2 * t + 1, 0)
        linear(h)
        window(h)
        return 0

    lax.fori_loop(0, 2, forward_meet, 0)
    lax.fori_loop(2, heads // 2, meet_two, 0)
    total, end = payload(cot[...], jnp.sum(acc[...], axis=0, keepdims=True), first_id)
    cbuf[0:feats, :] = total
    cbuf[feats : feats + TAIL, :] = end

    for j in range(1, share):
        send(cbuf, dbuf.at[j - 1], cs, cr.at[j - 1], beside(j))

    per = gq.shape[1]

    def head_of(turn):
        off = ((planes - turn) // 2) * (2 * (turn % 2) - 1)
        return lax.rem(row + off + planes, planes)

    def scatter(turn):
        h = head_of(turn)
        pltpu.make_async_copy(gq.at[h * share + col_x], xin.at[h, col_x], r1.at[h]).start()
        for j in range(1, share):
            to = h * share + lax.rem(col_x + j, share)
            send(gq.at[to], xin.at[h, col_x], s1, r1.at[h], beside(j))

    def row_sum(turn):
        h = head_of(turn)
        whole(xin.at[h], r1.at[h]).wait()
        return h, jnp.sum(xin[h].astype(F32), axis=0).astype(BF16)

    def climb(turn):
        h, part = row_sum(turn)
        zsend[h] = part
        send(zsend.at[h], zin.at[row], s2, r2, {"context": h * share + col_x})

    def backward(turn, _):
        h = head_of(turn)

        outs = []
        for i in range(0, length, step):
            end = i + step
            dn = dn_s[h, i:end, :]
            dd = dd_s[h, i:end, :]
            d_score = dot_nt(dn, vx[WIN : WIN + end, :]) + dd
            d_score = (d_score * mask[i:end, 0:end]).astype(BF16)
            d_phi = dot_nn(d_score, phik[0:end, :])
            d_phi += take[i:end, :] * (dot_nt(dn, state) + dd * norm)
            dphik[0:end, :] += dot_tn(d_score, phi_s[h, i:end, :])
            outs.append((d_phi * slope_s[h, i:end, :]).astype(BF16))
        grad = dot_tn(qb[h], jnp.concatenate(outs, axis=0)).astype(BF16)
        for j in range(share):
            gq[h * share + j] = grad[j * per : (j + 1) * per, :]
        return 0

    def backward_two(t, _):
        backward(2 * t, 0)
        return backward(2 * t + 1, 0)

    lax.fori_loop(0, SPLIT // 2, backward_two, 0)
    for turn in range(SPLIT):
        scatter(turn)
    backward_two(SPLIT // 2, 0)
    join_row(cbuf, dbuf, cr, tbuf, ebuf, es, er, last_id, False)
    scatter(SPLIT)
    scatter(SPLIT + 1)
    backward_two(SPLIT // 2 + 1, 0)
    scatter(SPLIT + 2)
    scatter(SPLIT + 3)
    for turn in range(SPLIT - 1):
        climb(turn)

    back, back_norm = from_rows(ebuf, er, last_id, False)
    own = jnp.where(columns_of(seg_ref[...]) == last_id, 1.0, 0.0)
    d_phi = dphik[...] + own * (dot_nt(vx[WIN : WIN + length, 0:width], back.astype(BF16)) + back_norm)
    d_pre = (d_phi * slopek[...]).astype(BF16)
    grad = dot_tn(kx[WIN : WIN + length, :], d_pre)
    kpart[...] = grad.reshape(kpart.shape).astype(BF16)

    def piece(ref, peer):
        return ref.at[lax.rem(peer["context"], share)]

    pltpu.make_async_copy(kpart.at[col_x], kxin.at[col_x], r4).start()
    for j in range(1, share):
        send(piece(kpart, beside(j)), kxin.at[col_x], s4, r4, beside(j))
    keys_out[...] = dot_nt(d_pre, fk[...]).astype(BF16)

    for turn in range(SPLIT - 1, heads - 1):
        climb(turn)
    zin[row] = row_sum(heads - 1)[1]
    whole(kxin, r4).wait()
    kmid[...] = jnp.sum(kxin[...].astype(F32), axis=0).astype(BF16)
    pltpu.make_async_copy(kmid, kzin.at[row], r5).start()
    for j in range(1, planes):
        send(kmid, kzin.at[row], s5, r5, along(j))
    whole(zin.at[pl.ds(0, planes - 1)], r2).wait()
    red[...] = jnp.sum(zin[...].astype(F32), axis=0).astype(BF16)
    pltpu.make_async_copy(red, spread.at[here], r3).start()
    for j in range(1, planes):
        send(red, spread.at[here], s3, ra.at[row], along(j))
    for j in range(1, share):
        send(red, spread.at[here], s7, r7, beside(j))

    def pass_on(off):
        source = lax.rem(row + off, planes)
        chunk = spread.at[source * share + col_x]
        whole(chunk, ra.at[source]).wait()
        for j in range(1, share):
            send(chunk, chunk, s7, r7, beside(j))

    order = sorted(range(1, planes), key=lambda o: min(o, planes - o))
    for off in order[:-3]:
        pass_on(off)
    whole(kzin, r5).wait()
    kred[...] = jnp.sum(kzin[...].astype(F32), axis=0).astype(BF16)
    pltpu.make_async_copy(kred, kspread.at[col_x], r6).start()
    for j in range(1, share):
        send(kred, kspread.at[col_x], s6, r6, beside(j))
    for off in order[-3:]:
        pass_on(off)

    for copy in sends:
        copy.wait_send()
    whole(qb.at[:, pl.ds(0, length - rows), :], qs).wait()
    whole(rbuf, xs).wait()
    whole(wbuf, us).wait()
    whole(dbuf, cs).wait()
    whole(ebuf, es).wait()
    whole(xin.at[:, pl.ds(0, share - 1)], s1).wait()
    whole(zin.at[pl.ds(0, planes - 1)], s2).wait()
    whole(spread.at[pl.ds(0, planes - 1)], s3).wait()
    whole(kxin.at[pl.ds(0, share - 1)], s4).wait()
    whole(kzin.at[pl.ds(0, planes - 1)], s5).wait()
    whole(kspread.at[pl.ds(0, share - 1)], s6).wait()
    beyond = spread.at[pl.ds(0, (share - 1) * planes)]
    whole(beyond, s7).wait()
    whole(spread.at[here], r3).wait()
    whole(kspread, r6).wait()
    whole(beyond, r7).wait()


def store_kernel(scale, err_in, keys_in, gq_in, gk_in, err_out, keys_out, gq_out, gk_out, gq, gk, sem):
    copies = [
        pltpu.make_async_copy(err_in, err_out, sem.at[0]),
        pltpu.make_async_copy(keys_in, keys_out, sem.at[1]),
        pltpu.make_async_copy(gq, gq_out, sem.at[2]),
        pltpu.make_async_copy(gk, gk_out, sem.at[3]),
    ]
    copies[0].start()
    copies[1].start()
    gk[...] = gk_in[...].astype(F32) * scale
    copies[3].start()
    gq[...] = gq_in[...].astype(F32) * scale
    copies[2].start()
    for copy in copies:
        copy.wait()


def on_device(queries, keys, values, segments, feat_q, feat_k):
    rows = keys.shape[0]
    split = lax.axis_size("ulysses")
    count = lax.axis_size("context")
    heads, width, feats = feat_q.shape
    length = rows * split
    seg = segments.reshape(1, length)
    key_map = feat_k.reshape(width, feats)
    per = heads * width // count
    share = count // heads
    planes = count // share
    shape = jax.ShapeDtypeStruct
    hbm = pl.BlockSpec(memory_space=pltpu.HBM)
    vmem = pl.BlockSpec(memory_space=pltpu.VMEM)
    dma = pltpu.SemaphoreType.DMA
    stay = functools.partial(pltpu.with_memory_space_constraint, memory_space=pltpu.HBM)
    ext = length + WIN
    packed = feats + TAIL

    outs = pl.pallas_call(
        step_kernel,
        name="step",
        out_shape=(
            shape((length, heads * width), BF16),
            shape((length, width), BF16),
            shape((count, per, feats), BF16),
            shape((share, width // share, feats), BF16),
        ),
        in_specs=[hbm] * 6,
        out_specs=[vmem] * 4,
        scratch_shapes=[
            pltpu.VMEM((1, length), jnp.int32),
            pltpu.VMEM((rows, queries.shape[1]), BF16),
            pltpu.VMEM((heads, length, width), BF16),
            pltpu.VMEM((ext, width), BF16),
            pltpu.VMEM((ext, width), BF16),
            pltpu.VMEM((heads, width, feats), BF16),
            pltpu.VMEM((width, feats), BF16),
            pltpu.VMEM((1, WIN), jnp.int32),
            pltpu.VMEM((packed, width), BF16),
            pltpu.VMEM((share - 1, packed, width), BF16),
            pltpu.VMEM((packed, width), BF16),
            pltpu.VMEM((share - 1, packed, width), BF16),
            pltpu.VMEM((packed, width), BF16),
            pltpu.VMEM((2, packed, width), BF16),
            pltpu.VMEM((packed, width), BF16),
            pltpu.VMEM((2, packed, width), BF16),
            pltpu.VMEM((feats, width), F32),
            pltpu.VMEM((8, feats), F32),
            pltpu.VMEM((length, length), F32),
            pltpu.VMEM((length, 2 * WIN), F32),
            pltpu.VMEM((length, feats), F32),
            pltpu.VMEM((length, feats), BF16),
            pltpu.VMEM((heads, length, feats), BF16),
            pltpu.VMEM((heads, length, feats), BF16),
            pltpu.VMEM((heads, length, feats), F32),
            pltpu.VMEM((heads, length, width), F32),
            pltpu.VMEM((heads, length, 1), F32),
            pltpu.VMEM((heads, length, width), F32),
            pltpu.VMEM((heads, length, width), BF16),
            pltpu.VMEM((heads, length, 1), F32),
            pltpu.VMEM((length, feats), BF16),
            pltpu.VMEM((length, feats), F32),
            pltpu.VMEM((length, feats), F32),
            pltpu.VMEM((feats, width), F32),
            pltpu.VMEM((8, feats), F32),
            pltpu.VMEM((count, per, feats), BF16),
            pltpu.VMEM((planes, share, per, feats), BF16),
            pltpu.VMEM((planes, per, feats), BF16),
            pltpu.VMEM((planes, per, feats), BF16),
            pltpu.VMEM((per, feats), BF16),
            pltpu.VMEM((share, per, feats), BF16),
            pltpu.VMEM((share, per, feats), BF16),
            pltpu.VMEM((per, feats), BF16),
            pltpu.VMEM((planes, per, feats), BF16),
            pltpu.VMEM((per, feats), BF16),
            dma,
            dma((3,)),
            dma((split - 1,)),
            dma((split - 1,)),
            dma,
            dma((split,)),
            dma((split,)),
            dma((heads,)),
            dma((3,)),
            dma((3,)),
            dma,
            dma((share - 1,)),
            dma,
            dma((share - 1,)),
            dma,
            dma((2,)),
            dma,
            dma((2,)),
        ]
        + [dma, dma((heads,))]
        + [dma] * 12
        + [dma((planes,))],
        compiler_params=pltpu.CompilerParams(
            collective_id=0, has_side_effects=True, vmem_limit_bytes=50 * 1024 * 1024
        ),
    )(stay(queries), stay(keys), stay(values), stay(seg), stay(feat_q), stay(key_map))

    errors, grad_keys, grad_q, grad_k = pl.pallas_call(
        functools.partial(store_kernel, 1.0 / math.sqrt(length * count)),
        name="store",
        out_shape=(
            shape((length, heads * width), BF16),
            shape((length, width), BF16),
            shape((count, per, feats), F32),
            shape((share, width // share, feats), F32),
        ),
        in_specs=[vmem] * 4,
        out_specs=[hbm] * 4,
        scratch_shapes=[
            pltpu.VMEM((count, per, feats), F32),
            pltpu.VMEM((share, width // share, feats), F32),
            dma((4,)),
        ],
        compiler_params=pltpu.CompilerParams(vmem_limit_bytes=8 * 1024 * 1024),
    )(*outs)
    return (
        errors,
        grad_keys,
        grad_q.reshape(heads, width, feats),
        grad_k.reshape(feat_k.shape),
    )


def solution(mesh):
    in_specs = (
        P(("dp", "context", "ulysses"), None),
        P(("dp", "context", "ulysses"), None),
        P(("dp", "context", "ulysses"), None),
        P(("dp", "context")),
        P("ulysses", None, None),
        P("ulysses", None, None),
    )
    out_specs = (
        P(("dp", "context"), "ulysses"),
        P(("dp", "context"), "ulysses"),
        P(("dp", "ulysses"), None, None),
        P(("dp", "ulysses"), None, None),
    )
    return jax.shard_map(
        on_device, mesh=mesh, in_specs=in_specs, out_specs=out_specs, check_vma=False
    )
```

```python
import functools
import math

import jax
import jax.numpy as jnp
from jax import lax
from jax.experimental import pallas as pl
from jax.experimental.pallas import tpu as pltpu
from jax.sharding import PartitionSpec as P

WIN = 128
JOIN = 3
SPLIT = 4
TAIL = 16
MESH = pl.DeviceIdType.MESH
F32 = jnp.float32
BF16 = jnp.bfloat16


def dot_nn(a, b):
    return lax.dot_general(a, b, (((1,), (0,)), ((), ())), preferred_element_type=F32)


def dot_nt(a, b):
    return lax.dot_general(a, b, (((1,), (1,)), ((), ())), preferred_element_type=F32)


def dot_tn(a, b):
    return lax.dot_general(a, b, (((0,), (0,)), ((), ())), preferred_element_type=F32)


def remote(src, dst, send, recv, **where):
    return pltpu.make_async_remote_copy(
        src_ref=src, dst_ref=dst, send_sem=send, recv_sem=recv, device_id=where, device_id_type=MESH
    )


def whole(ref, sem):
    return pltpu.make_async_copy(ref, ref, sem)


def columns_of(seg_row):
    length = seg_row.shape[1]
    parts = [
        jnp.transpose(jnp.broadcast_to(seg_row[:, i : i + 128].astype(F32), (128, 128)))
        for i in range(0, length, 128)
    ]
    return jnp.concatenate(parts, axis=0)


def payload(state, norm, ident):
    row = lax.broadcasted_iota(jnp.int32, (TAIL, norm.shape[1]), 0)
    tail = jnp.where(row == 0, norm, jnp.where(row == 1, ident, 0.0))
    return state.astype(BF16), tail.astype(BF16)


def step_kernel(
    q_ref, k_ref, v_ref, seg_in, fq_ref, fk_ref,
    err_ref, keys_out, spread, kspread,
    seg_ref, qv, qb, kx, vx, fq, fk, rim_in, sbuf, rbuf, cbuf, dbuf, tbuf, ebuf, ubuf, wbuf, back_s, backn_s,
    mask, bias, take, takeb, own_s, lead_s, phi_s, slope_s, num_s, den_s, tea_s, dn_s, dd_s, phik, slopek, dphik, cot, acc,
    gq, xin, zsend, zin, red, kpart, kxin, kmid, kzin, kred,
    ql, fl, ks, vs, qs, kr, vr, qr, rs, rr, xs, xr, cs, cr, es, er, us, ur,
    s1, r1, s2, r2, s3, r3, s4, r4, s5, r5, s6, r6, s7, r7, ra,
):
    here, mine = lax.axis_index("context"), lax.axis_index("ulysses")
    count, split = lax.axis_size("context"), lax.axis_size("ulysses")
    rows = k_ref.shape[0]
    heads, width, feats = fq_ref.shape
    length = rows * split
    wide = heads * width
    step = 256
    inv_scale = 1.0 / math.sqrt(width)

    share = count // heads
    row, col_x = here // share, lax.rem(here, share)
    planes = count // share

    def beside(j):
        return {"context": row * share + lax.rem(col_x + j, share)}

    def along(j):
        return {"context": lax.rem(row + j, planes) * share + col_x}

    barrier = pltpu.get_barrier_semaphore()
    near = [{"ulysses": lax.rem(mine + j, split)} for j in range(1, split)]
    near += [beside(j) for j in range(1, share)]
    near += [along(j) for j in range(1, planes)]
    near += [{"context": lax.rem(here + k, count)} for k in (1, count - 1)]
    for peer in near:
        pl.semaphore_signal(barrier, inc=1, device_id=peer, device_id_type=MESH)

    def place(start):
        return pl.ds(pl.multiple_of(start + mine * rows, 128), rows)

    def lanes(who, size):
        return pl.ds(pl.multiple_of(who * size, 128), size)

    load_seg = pltpu.make_async_copy(seg_in, seg_ref, fl.at[2])
    load_seg.start()
    front = pl.ds(0, width)
    small = ((k_ref, kx, ks, kr), (v_ref, vx, vs, vr))
    for src, dst, _, recv in small:
        pltpu.make_async_copy(
            src.at[:, lanes(mine, width)], dst.at[place(WIN), front], recv.at[mine]
        ).start()
    load_q = pltpu.make_async_copy(q_ref, qv, ql)
    load_q.start()
    loads = [pltpu.make_async_copy(fq_ref, fq, fl.at[0]), pltpu.make_async_copy(fk_ref, fk, fl.at[1])]
    for copy in loads:
        copy.start()

    pl.semaphore_wait(barrier, len(near))

    sends = []
    for src, dst, send, recv in small:
        for j in range(1, split):
            peer = lax.rem(mine + j, split)
            copy = remote(
                src.at[:, lanes(peer, width)], dst.at[place(WIN), front], send.at[j - 1],
                recv.at[mine], ulysses=peer,
            )
            copy.start()
            sends.append(copy)

    load_q.wait()
    for h in range(heads):
        pltpu.make_async_copy(
            qv.at[:, lanes(mine * heads + h, width)], qb.at[h, place(0), :], qr.at[h]
        ).start()

    def send_q(h, _):
        for j in range(1, split):
            peer = lax.rem(mine + j, split)
            remote(
                qv.at[:, lanes(peer * heads + h, width)], qb.at[h, place(0), :], qs, qr.at[h],
                ulysses=peer,
            ).start()
        return 0

    lax.fori_loop(0, heads, send_q, 0)

    load_seg.wait()
    seg_row = seg_ref[...]
    rows_f = seg_row.astype(F32)
    first_id = jnp.min(seg_row, axis=1, keepdims=True).astype(F32)
    last_id = jnp.max(seg_row, axis=1, keepdims=True).astype(F32)
    seg_col = columns_of(seg_row)
    take[...] = jnp.where(seg_col == first_id, 1.0, 0.0)
    own_s[...] = jnp.where(seg_col == last_id, 1.0, 0.0)
    takeb[...] = jnp.where(seg_col == first_id, 1.0, 0.0).astype(BF16)
    r = lax.broadcasted_iota(jnp.int32, (128, 128), 0)
    c = lax.broadcasted_iota(jnp.int32, (128, 128), 1)
    for i in range(0, length, 128):
        col = seg_col[i : i + 128, :]
        for j in range(0, length, 128):
            if j > i:
                mask[i : i + 128, j : j + 128] = jnp.zeros((128, 128), F32)
                continue
            same = col == rows_f[:, j : j + 128]
            if j == i:
                same = same & (c <= r)
            mask[i : i + 128, j : j + 128] = jnp.where(same, 1.0, 0.0)
        if i:
            bias[i : i + 128, 0:128] = jnp.where(
                (col == rows_f[:, i - 128 : i]) & (c > r), 0.0, -1e30
            )
        bias[i : i + 128, 128:256] = jnp.where(
            (col == rows_f[:, i : i + 128]) & (c <= r), 0.0, -1e30
        )
    cot[...] = jnp.zeros_like(cot)
    acc[...] = jnp.zeros_like(acc)
    dphik[...] = jnp.zeros_like(dphik)
    for copy in loads:
        copy.wait()
    after = lax.rem(here + 1, count)
    edge, rim = pl.ds(length, WIN), pl.ds(0, WIN)
    rims = [
        remote(seg_ref.at[:, pl.ds(length - WIN, WIN)], rim_in, rs.at[2], rr.at[2], context=after),
        remote(kx.at[edge, front], kx.at[rim, front], rs.at[0], rr.at[0], context=after),
        remote(vx.at[edge, front], vx.at[rim, front], rs.at[1], rr.at[1], context=after),
    ]
    rims[0].start()

    def arrived(ref, sems, who):
        whole(ref.at[pl.ds(WIN + who * rows, rows), front], sems.at[who]).wait()

    arrived(kx, kr, split - 1)
    rims[1].start()
    arrived(vx, vr, split - 1)
    rims[2].start()
    for who in range(split - 1):
        arrived(kx, kr, who)
    for who in range(split - 1):
        arrived(vx, vr, who)

    pre = dot_nn(kx[WIN : WIN + length, :], fk[...])
    low = jnp.exp(jnp.minimum(pre, 0.0))
    phi = jnp.where(pre > 0, pre + 1.0, low).astype(BF16)
    phik[...] = phi
    slopek[...] = jnp.where(pre > 0, 1.0, low)
    tail = jnp.where(seg_col == last_id, phi.astype(F32), 0.0)
    state, end = payload(
        dot_tn(tail.astype(BF16), vx[WIN : WIN + length, 0:width]),
        jnp.sum(tail, axis=0, keepdims=True),
        last_id,
    )
    sbuf[0:feats, :] = state
    sbuf[feats : feats + TAIL, :] = end
    def send(src, dst, send_sem, recv_sem, peer):
        pltpu.make_async_remote_copy(
            src_ref=src, dst_ref=dst, send_sem=send_sem, recv_sem=recv_sem,
            device_id=peer, device_id_type=MESH,
        ).start()

    def opened(ref):
        tail = ref[feats : feats + TAIL, :].astype(F32)
        return ref[0:feats, :].astype(F32), tail[0:1, :], tail[1:2, :]

    def join_row(own, buf, sems, out, far, out_sem, far_sems, ident, ahead):
        for j in range(share - 1):
            whole(buf.at[j], sems.at[j]).wait()
        parts = [opened(buf.at[j]) for j in range(share - 1)]
        every = parts + [opened(own)]
        lead_id = every[0][2]
        for part in every[1:]:
            lead_id = jnp.maximum(lead_id, part[2]) if ahead else jnp.minimum(lead_id, part[2])
        sums = [jnp.where(p[2] == lead_id, p[0], 0.0) for p in every]
        norms = [jnp.where(p[2] == lead_id, p[1], 0.0) for p in every]
        total, end = payload(sum(sums), sum(norms), lead_id)
        out[0:feats, :] = total
        out[feats : feats + TAIL, :] = end
        for k in range(2):
            send(out, far.at[k], out_sem, far_sems.at[k], along(k + 1 if ahead else planes - 1 - k))
        got, got_norm = jnp.zeros((feats, width), F32), jnp.zeros((1, feats), F32)
        for j in range(share - 1):
            source = lax.rem(col_x + share - 1 - j, share)
            side = source < col_x if ahead else source > col_x
            keep = (parts[j][2] == ident) & side
            got += jnp.where(keep, parts[j][0], 0.0)
            got_norm += jnp.where(keep, parts[j][1], 0.0)
        back_s[...] = got
        backn_s[...] = jnp.broadcast_to(got_norm, backn_s.shape)

    def from_rows(far, far_sems, ident, ahead):
        got, got_norm = back_s[...], backn_s[0:1, :]
        for k in range(2):
            whole(far.at[k], far_sems.at[k]).wait()
            part = opened(far.at[k])
            inside = row > k if ahead else row + k + 1 < planes
            keep = (part[2] == ident) & inside
            got += jnp.where(keep, part[0], 0.0)
            got_norm += jnp.where(keep, part[1], 0.0)
        return got, got_norm

    for j in range(1, share):
        send(sbuf, rbuf.at[j - 1], xs, xr.at[j - 1], beside(j))

    def linear(h):
        q = qb[h]
        pre = dot_nn(q, fq[h])
        low = jnp.exp(jnp.minimum(pre, 0.0))
        phi = jnp.where(pre > 0, pre + 1.0, low).astype(BF16)
        slope_s[h] = jnp.where(pre > 0, 1.0, low)
        phi_s[h] = phi
        lead_s[h] = phi * takeb[...]
        for i in range(0, length, step):
            end = i + step
            score = dot_nt(phi[i:end], phik[0:end, :]) * mask[i:end, 0:end]
            num_s[h, i:end, :] = dot_nn(score.astype(BF16), vx[WIN : WIN + end, :])
            den_s[h, i:end, :] = jnp.sum(score, axis=1, keepdims=True)

    def window(h):
        q = qb[h]
        for j in range(0, length, 128):
            logits = dot_nt(q[j : j + 128], kx[j : j + 256, :]) * inv_scale
            logits += bias[j : j + 128, :]
            probs = jnp.exp(logits - jnp.max(logits, axis=1, keepdims=True))
            total = jnp.sum(probs, axis=1, keepdims=True)
            tea_s[h, j : j + 128, :] = dot_nn(probs.astype(BF16), vx[j : j + 256, :]) * (1.0 / total)

    def forward(h, _):
        whole(qb.at[h], qr.at[h]).wait()
        linear(h)
        window(h)
        return 0

    for h in range(2):
        whole(qb.at[h], qr.at[h]).wait()
        linear(h)
    for copy in rims:
        copy.wait()
    rim_f = jnp.where(here > 0, rim_in[...], -1).astype(F32)
    bias[0:128, 0:128] = jnp.where((seg_col[0:128, :] == rim_f) & (c > r), 0.0, -1e30)

    for h in range(2):
        window(h)
    lax.fori_loop(2, JOIN, forward, 0)
    join_row(sbuf, rbuf, xr, ubuf, wbuf, us, ur, first_id, True)
    lax.fori_loop(JOIN, heads - 2, forward, 0)
    state, norm = from_rows(wbuf, ur, first_id, True)
    state = state.astype(BF16)

    def meet(h, _):
        lead = lead_s[h]
        lead_f = lead.astype(F32)
        inv = 1.0 / (den_s[h] + jnp.sum(lead_f * norm, axis=1, keepdims=True))
        student = (num_s[h] + dot_nn(lead, state)) * inv
        gap = student - tea_s[h]
        err_ref[:, lanes(h, width)] = gap.astype(BF16)
        up = 32.0 * gap
        dn = (up * inv).astype(BF16)
        dd = -jnp.sum(up * student, axis=1, keepdims=True) * inv
        dn_s[h] = dn
        dd_s[h] = dd
        acc[...] += jnp.sum((lead_f * dd).reshape(length // 8, 8, feats), axis=0)
        cot[...] += dot_tn(lead, dn)
        return 0

    def meet_two(t, _):
        meet(2 * t, 0)
        return meet(2 * t + 1, 0)

    def forward_meet(t, _):
        h = heads - 2 + t
        meet(2 * t, 0)
        whole(qb.at[h], qr.at[h]).wait()
        meet(2 * t + 1, 0)
        linear(h)
        window(h)
        return 0

    lax.fori_loop(0, 2, forward_meet, 0)
    lax.fori_loop(2, heads // 2, meet_two, 0)
    total, end = payload(cot[...], jnp.sum(acc[...], axis=0, keepdims=True), first_id)
    cbuf[0:feats, :] = total
    cbuf[feats : feats + TAIL, :] = end

    for j in range(1, share):
        send(cbuf, dbuf.at[j - 1], cs, cr.at[j - 1], beside(j))

    per = gq.shape[1]

    def head_of(turn):
        off = ((planes - turn) // 2) * (2 * (turn % 2) - 1)
        return lax.rem(row + off + planes, planes)

    def scatter(turn):
        h = head_of(turn)
        pltpu.make_async_copy(gq.at[h * share + col_x], xin.at[h, col_x], r1.at[h]).start()
        for j in range(1, share):
            to = h * share + lax.rem(col_x + j, share)
            send(gq.at[to], xin.at[h, col_x], s1, r1.at[h], beside(j))

    def row_sum(turn):
        h = head_of(turn)
        whole(xin.at[h], r1.at[h]).wait()
        return h, jnp.sum(xin[h].astype(F32), axis=0).astype(BF16)

    def climb(turn):
        h, part = row_sum(turn)
        zsend[h] = part
        send(zsend.at[h], zin.at[row], s2, r2, {"context": h * share + col_x})

    def backward(turn, _):
        h = head_of(turn)

        outs = []
        for i in range(0, length, step):
            end = i + step
            dn = dn_s[h, i:end, :]
            dd = dd_s[h, i:end, :]
            d_score = dot_nt(dn, vx[WIN : WIN + end, :]) + dd
            d_score = (d_score * mask[i:end, 0:end]).astype(BF16)
            d_phi = dot_nn(d_score, phik[0:end, :])
            d_phi += take[i:end, :] * (dot_nt(dn, state) + dd * norm)
            dphik[0:end, :] += dot_tn(d_score, phi_s[h, i:end, :])
            outs.append((d_phi * slope_s[h, i:end, :]).astype(BF16))
        grad = dot_tn(qb[h], jnp.concatenate(outs, axis=0)).astype(BF16)
        for j in range(share):
            gq[h * share + j] = grad[j * per : (j + 1) * per, :]
        return 0

    def backward_two(t, _):
        backward(2 * t, 0)
        return backward(2 * t + 1, 0)

    lax.fori_loop(0, SPLIT // 2, backward_two, 0)
    for turn in range(SPLIT):
        scatter(turn)
    backward_two(SPLIT // 2, 0)
    join_row(cbuf, dbuf, cr, tbuf, ebuf, es, er, last_id, False)
    scatter(SPLIT)
    scatter(SPLIT + 1)
    backward_two(SPLIT // 2 + 1, 0)
    scatter(SPLIT + 2)
    scatter(SPLIT + 3)
    for turn in range(SPLIT - 1):
        climb(turn)

    back, back_norm = from_rows(ebuf, er, last_id, False)
    own = own_s[...]
    d_phi = dphik[...] + own * (dot_nt(vx[WIN : WIN + length, 0:width], back.astype(BF16)) + back_norm)
    d_pre = (d_phi * slopek[...]).astype(BF16)
    grad = dot_tn(kx[WIN : WIN + length, :], d_pre)
    kpart[...] = grad.reshape(kpart.shape).astype(BF16)

    def piece(ref, peer):
        return ref.at[lax.rem(peer["context"], share)]

    pltpu.make_async_copy(kpart.at[col_x], kxin.at[col_x], r4).start()
    for j in range(1, share):
        send(piece(kpart, beside(j)), kxin.at[col_x], s4, r4, beside(j))
    keys_out[...] = dot_nt(d_pre, fk[...]).astype(BF16)

    for turn in range(SPLIT - 1, heads - 1):
        climb(turn)
    zin[row] = row_sum(heads - 1)[1]
    whole(kxin, r4).wait()
    kmid[...] = jnp.sum(kxin[...].astype(F32), axis=0).astype(BF16)
    pltpu.make_async_copy(kmid, kzin.at[row], r5).start()
    for j in range(1, planes):
        send(kmid, kzin.at[row], s5, r5, along(j))
    whole(zin.at[pl.ds(0, planes - 1)], r2).wait()
    red[...] = jnp.sum(zin[...].astype(F32), axis=0).astype(BF16)
    pltpu.make_async_copy(red, spread.at[here], r3).start()
    for j in range(1, planes):
        send(red, spread.at[here], s3, ra.at[row], along(j))
    for j in range(1, share):
        send(red, spread.at[here], s7, r7, beside(j))

    def pass_on(off):
        source = lax.rem(row + off, planes)
        chunk = spread.at[source * share + col_x]
        whole(chunk, ra.at[source]).wait()
        for j in range(1, share):
            send(chunk, chunk, s7, r7, beside(j))

    order = sorted(range(1, planes), key=lambda o: min(o, planes - o))
    for off in order[:-3]:
        pass_on(off)
    whole(kzin, r5).wait()
    kred[...] = jnp.sum(kzin[...].astype(F32), axis=0).astype(BF16)
    pltpu.make_async_copy(kred, kspread.at[col_x], r6).start()
    for j in range(1, share):
        send(kred, kspread.at[col_x], s6, r6, beside(j))
    for off in order[-3:]:
        pass_on(off)

    for copy in sends:
        copy.wait_send()
    whole(qb.at[:, pl.ds(0, length - rows), :], qs).wait()
    whole(rbuf, xs).wait()
    whole(wbuf, us).wait()
    whole(dbuf, cs).wait()
    whole(ebuf, es).wait()
    whole(xin.at[:, pl.ds(0, share - 1)], s1).wait()
    whole(zin.at[pl.ds(0, planes - 1)], s2).wait()
    whole(spread.at[pl.ds(0, planes - 1)], s3).wait()
    whole(kxin.at[pl.ds(0, share - 1)], s4).wait()
    whole(kzin.at[pl.ds(0, planes - 1)], s5).wait()
    whole(kspread.at[pl.ds(0, share - 1)], s6).wait()
    beyond = spread.at[pl.ds(0, (share - 1) * planes)]
    whole(beyond, s7).wait()
    whole(spread.at[here], r3).wait()
    whole(kspread, r6).wait()
    whole(beyond, r7).wait()


def store_kernel(scale, err_in, keys_in, gq_in, gk_in, err_out, keys_out, gq_out, gk_out, gq, gk, sem):
    copies = [
        pltpu.make_async_copy(err_in, err_out, sem.at[0]),
        pltpu.make_async_copy(keys_in, keys_out, sem.at[1]),
        pltpu.make_async_copy(gq, gq_out, sem.at[2]),
        pltpu.make_async_copy(gk, gk_out, sem.at[3]),
    ]
    copies[0].start()
    copies[1].start()
    gk[...] = gk_in[...].astype(F32) * scale
    copies[3].start()
    gq[...] = gq_in[...].astype(F32) * scale
    copies[2].start()
    for copy in copies:
        copy.wait()


def on_device(queries, keys, values, segments, feat_q, feat_k):
    rows = keys.shape[0]
    split = lax.axis_size("ulysses")
    count = lax.axis_size("context")
    heads, width, feats = feat_q.shape
    length = rows * split
    seg = segments.reshape(1, length)
    key_map = feat_k.reshape(width, feats)
    per = heads * width // count
    share = count // heads
    planes = count // share
    shape = jax.ShapeDtypeStruct
    hbm = pl.BlockSpec(memory_space=pltpu.HBM)
    vmem = pl.BlockSpec(memory_space=pltpu.VMEM)
    dma = pltpu.SemaphoreType.DMA
    stay = functools.partial(pltpu.with_memory_space_constraint, memory_space=pltpu.HBM)
    ext = length + WIN
    packed = feats + TAIL

    outs = pl.pallas_call(
        step_kernel,
        name="step",
        out_shape=(
            shape((length, heads * width), BF16),
            shape((length, width), BF16),
            shape((count, per, feats), BF16),
            shape((share, width // share, feats), BF16),
        ),
        in_specs=[hbm] * 6,
        out_specs=[vmem] * 4,
        scratch_shapes=[
            pltpu.VMEM((1, length), jnp.int32),
            pltpu.VMEM((rows, queries.shape[1]), BF16),
            pltpu.VMEM((heads, length, width), BF16),
            pltpu.VMEM((ext, width), BF16),
            pltpu.VMEM((ext, width), BF16),
            pltpu.VMEM((heads, width, feats), BF16),
            pltpu.VMEM((width, feats), BF16),
            pltpu.VMEM((1, WIN), jnp.int32),
            pltpu.VMEM((packed, width), BF16),
            pltpu.VMEM((share - 1, packed, width), BF16),
            pltpu.VMEM((packed, width), BF16),
            pltpu.VMEM((share - 1, packed, width), BF16),
            pltpu.VMEM((packed, width), BF16),
            pltpu.VMEM((2, packed, width), BF16),
            pltpu.VMEM((packed, width), BF16),
            pltpu.VMEM((2, packed, width), BF16),
            pltpu.VMEM((feats, width), F32),
            pltpu.VMEM((8, feats), F32),
            pltpu.VMEM((length, length), F32),
            pltpu.VMEM((length, 2 * WIN), F32),
            pltpu.VMEM((length, feats), F32),
            pltpu.VMEM((length, feats), BF16),
            pltpu.VMEM((length, feats), F32),
            pltpu.VMEM((heads, length, feats), BF16),
            pltpu.VMEM((heads, length, feats), BF16),
            pltpu.VMEM((heads, length, feats), F32),
            pltpu.VMEM((heads, length, width), F32),
            pltpu.VMEM((heads, length, 1), F32),
            pltpu.VMEM((heads, length, width), F32),
            pltpu.VMEM((heads, length, width), BF16),
            pltpu.VMEM((heads, length, 1), F32),
            pltpu.VMEM((length, feats), BF16),
            pltpu.VMEM((length, feats), F32),
            pltpu.VMEM((length, feats), F32),
            pltpu.VMEM((feats, width), F32),
            pltpu.VMEM((8, feats), F32),
            pltpu.VMEM((count, per, feats), BF16),
            pltpu.VMEM((planes, share, per, feats), BF16),
            pltpu.VMEM((planes, per, feats), BF16),
            pltpu.VMEM((planes, per, feats), BF16),
            pltpu.VMEM((per, feats), BF16),
            pltpu.VMEM((share, per, feats), BF16),
            pltpu.VMEM((share, per, feats), BF16),
            pltpu.VMEM((per, feats), BF16),
            pltpu.VMEM((planes, per, feats), BF16),
            pltpu.VMEM((per, feats), BF16),
            dma,
            dma((3,)),
            dma((split - 1,)),
            dma((split - 1,)),
            dma,
            dma((split,)),
            dma((split,)),
            dma((heads,)),
            dma((3,)),
            dma((3,)),
            dma,
            dma((share - 1,)),
            dma,
            dma((share - 1,)),
            dma,
            dma((2,)),
            dma,
            dma((2,)),
        ]
        + [dma, dma((heads,))]
        + [dma] * 12
        + [dma((planes,))],
        compiler_params=pltpu.CompilerParams(
            collective_id=0, has_side_effects=True, vmem_limit_bytes=50 * 1024 * 1024,
        ),
    )(stay(queries), stay(keys), stay(values), stay(seg), stay(feat_q), stay(key_map))

    errors, grad_keys, grad_q, grad_k = pl.pallas_call(
        functools.partial(store_kernel, 1.0 / math.sqrt(length * count)),
        name="store",
        out_shape=(
            shape((length, heads * width), BF16),
            shape((length, width), BF16),
            shape((count, per, feats), F32),
            shape((share, width // share, feats), F32),
        ),
        in_specs=[vmem] * 4,
        out_specs=[hbm] * 4,
        scratch_shapes=[
            pltpu.VMEM((count, per, feats), F32),
            pltpu.VMEM((share, width // share, feats), F32),
            dma((4,)),
        ],
        compiler_params=pltpu.CompilerParams(vmem_limit_bytes=8 * 1024 * 1024),
    )(*outs)
    return (
        errors,
        grad_keys,
        grad_q.reshape(heads, width, feats),
        grad_k.reshape(feat_k.shape),
    )


def solution(mesh):
    in_specs = (
        P(("dp", "context", "ulysses"), None),
        P(("dp", "context", "ulysses"), None),
        P(("dp", "context", "ulysses"), None),
        P(("dp", "context")),
        P("ulysses", None, None),
        P("ulysses", None, None),
    )
    out_specs = (
        P(("dp", "context"), "ulysses"),
        P(("dp", "context"), "ulysses"),
        P(("dp", "ulysses"), None, None),
        P(("dp", "ulysses"), None, None),
    )
    return jax.shard_map(
        on_device, mesh=mesh, in_specs=in_specs, out_specs=out_specs, check_vma=False
    )
```
